32 devices in a mesh: parts: 2 (over y), space: 16 (over z, x, core).
Axes of the slice: x: 2, y: 2, z: 4, core: 2. Of those that a mesh axis runs over, the one named last changes fastest.
Arguments:
- outer_grad: bfloat16 [32, 4, 128, 1024], P(('parts', 'space')), parts along dimension 0, may hold values from -6 to 6
- block_input: bfloat16 [32, 4, 128, 1024], P(('parts', 'space')), parts along dimension 0, may hold values from -6 to 6
- third_input: bfloat16 [32, 4, 128, 1024], P(('parts', 'space')), parts along dimension 0, as said below
- second_input: bfloat16 [32, 8, 256, 256], P(('parts', 'space')), parts along dimension 0, as said below
- third_weight: bfloat16 [1024, 1024], replicated, may hold values from -0.1875 to 0.1875
- group_weight: bfloat16 [1024, 288], replicated, may hold values from -0.375 to 0.375
- first_weight: bfloat16 [1024, 1024], replicated, may hold values from -0.1875 to 0.1875
Outputs:
- input_grad: bfloat16 [32, 4, 128, 1024], P(('parts', 'space')), parts along dimension 0
- third_wgrad: float32 [2048, 1024], P(('parts', 'space')), parts along dimension 0
- group_wgrad: float32 [2048, 288], P(('parts', 'space')), parts along dimension 0
- first_wgrad: float32 [2048, 1024], P(('parts', 'space')), parts along dimension 0
The draws below stay inside these ranges and needn't reach their ends.
There are 2 independent parts, one for each index of `parts`. The reference program is written for one: setup_inputs(seed, part) draws one part's arguments, and reference() takes and returns one part's arrays. A program takes and returns all parts, laid end to end along the dimension named above; an argument that names none is the same for every part. Nothing has to cross between parts.
Inputs may be any that keep to these rules, and one draw needn't show every extreme that they name: `third_input`: rectified values: zero or positive, about half of them zero. `second_input`: rectified values: zero or positive, about half of them zero.
All inputs are finite; a program needn't handle non-finite values.
Results may differ from the reference program's by a relative error of at most 0.0049.
Values may be sent and summed in bfloat16 or wider, within the bound.
A program may use at most 128 MiB of HBM per device.

```python
import math
import jax
import jax.numpy as jnp

C = 1024
GROUPS = 32
BH = 4
BW = 128
GW = 32
CS = 256
GRID_ROWS = 4
HEIGHT = 32
WIDTH = 256
POSITIONS = 8192
N_SPACE = 16


def rectified(key, shape):
    base_key, factor_key = jax.random.split(key)
    base = jnp.clip(jax.random.normal(base_key, shape, jnp.float32), -6.0, 6.0)
    factor = jnp.exp(jax.random.uniform(factor_key, shape, jnp.float32, math.log(0.5), math.log(2.0)))
    return (jnp.maximum(base, 0.0) * factor).astype(jnp.bfloat16)


def draw_third_input(key, part):
    return rectified(jax.random.fold_in(key, 31), (N_SPACE, BH, BW, C))


def draw_second_input(key, part):
    return rectified(jax.random.fold_in(key, 57), (N_SPACE, 2 * BH, 2 * BW, CS))


def raised(array, stream_key, source, target, shards_of, factor):
    owner, partner = [(jnp.arange(array.shape[position]) // (array.shape[position] // shards_of)).reshape([-1 if axis == position else 1 for axis in range(array.ndim)]) for position in (source, target)]
    chosen = jax.random.permutation(stream_key, shards_of)[partner]
    strong = (owner == chosen) | (owner == (partner + shards_of // 2) % shards_of)
    return jnp.where(strong, factor * array, array)


def block_scale(stream_key, extent, shards, smallest, largest):
    factor_of = 1.0
    for axis_at, blocks in shards:
        steps = jax.random.uniform(jax.random.fold_in(jax.random.fold_in(stream_key, 6), axis_at), (blocks,), jnp.float32, smallest / len(shards), largest / len(shards))
        factor_of = factor_of * jnp.repeat(jnp.exp(steps), extent[axis_at] // blocks).reshape((-1,) + (1,) * (len(extent) - 1 - axis_at))
    return factor_of


def noise(key, shape, deviation, bound, pieces=(), dtype=jnp.bfloat16):
    drawn = jax.random.normal(key, shape, jnp.float32) * deviation
    if len(pieces) > 0:
        drawn = block_scale(key, shape, pieces, -0.22, 0.18) * drawn
    return jnp.clip(drawn, min=-bound, max=bound).astype(dtype)


def bell_draw_with(own_key, dims, deviation, most, cuts, heavy, dtype=jnp.bfloat16):
    array = deviation * jax.random.normal(own_key, dims, jnp.float32)
    if cuts:
        array = array * block_scale(own_key, dims, cuts, -0.22, 0.18)
    return jnp.clip(raised(array, jax.random.fold_in(own_key, 3), *heavy), -most, most).astype(dtype)


def setup_inputs(seed: int = 0, part: int = 0) -> dict:
    key_of = jax.random.split(jax.random.key(seed), 8)
    part_keys = jax.random.split(jax.random.fold_in(key_of[7], part), 8)
    outer_grad = noise(part_keys[0], (N_SPACE, BH, BW, C), 1.0, 6.0, ((0, 16),))
    block_input = bell_draw_with(part_keys[1], (N_SPACE, BH, BW, C), 1.0, 6.0, ((0, 16),), (0, 3, 16, 2.0))
    third_input = draw_third_input(jax.random.fold_in(jax.random.fold_in(key_of[7], part), 71), part)
    second_input = draw_second_input(jax.random.fold_in(jax.random.fold_in(key_of[7], part), 71), part)
    third_weight = noise(key_of[4], (C, C), C ** -0.5, 0.1875)
    group_weight = noise(key_of[5], (C, 9 * GW), (9 * GW) ** -0.5, 0.375)
    first_weight = noise(key_of[6], (C, C), C ** -0.5, 0.1875)
    return dict(outer_grad=outer_grad, block_input=block_input, third_input=third_input, second_input=second_input, third_weight=third_weight, group_weight=group_weight, first_weight=first_weight)


def tiles_image(tiles):
    grid_rows = 2 * GRID_ROWS
    return tiles.reshape(grid_rows, 2, BH, BW, C).transpose(0, 2, 1, 3, 4).reshape(grid_rows * BH, 2 * BW, C)

def image_tiles(image):
    grid_rows = 2 * GRID_ROWS
    return image.reshape(grid_rows, BH, 2, BW, C).transpose(0, 2, 1, 3, 4).reshape(N_SPACE, BH, BW, C)

def blocks_image(blocks):
    shaped = blocks.reshape(GRID_ROWS, 2, 2, 2 * BH, 2 * BW, CS)
    return shaped.transpose(0, 3, 4, 1, 2, 5).reshape(HEIGHT, WIDTH, C)

def reference(outer_grad, block_input, third_input, second_input, third_weight, group_weight, first_weight):
    normalizer = 1.0 / math.sqrt(POSITIONS)
    grad_rows = tiles_image(outer_grad).reshape(POSITIONS, C)
    third_rows = tiles_image(third_input).reshape(POSITIONS, C)
    input_rows = tiles_image(block_input).reshape(POSITIONS, C)
    second_map = blocks_image(second_input)
    back_third = jnp.dot(grad_rows, third_weight.T, preferred_element_type=jnp.float32)
    inner_grad = jnp.where(third_rows > 0, back_third, 0.0).astype(jnp.bfloat16)
    third_wgrad = jnp.dot(third_rows.T, grad_rows, preferred_element_type=jnp.float32) * normalizer
    padded = jnp.pad(inner_grad.reshape(HEIGHT, WIDTH, C).astype(jnp.float32), ((1, 1), (1, 1), (0, 0)))
    kernel = group_weight.astype(jnp.float32).reshape(GROUPS, GW, 9, GW)
    second_groups = second_map.astype(jnp.float32).reshape(HEIGHT, WIDTH, GROUPS, GW)
    back_second = jnp.zeros((HEIGHT, WIDTH, GROUPS, GW), jnp.float32)
    tap_terms = []
    for tap_row in range(3):
        for tap_col in range(3):
            window = padded[2 - tap_row:2 - tap_row + HEIGHT, 2 - tap_col:2 - tap_col + WIDTH].reshape(HEIGHT, WIDTH, GROUPS, GW)
            back_second = back_second + jnp.einsum('hwgo,goi->hwgi', window, kernel[:, :, 3 * tap_row + tap_col, :])
            tap_terms.append(jnp.einsum('hwgi,hwgo->goi', second_groups, window))
    group_wgrad = jnp.stack(tap_terms, 2).reshape(C, 9 * GW) * normalizer
    first_map = jnp.where(second_map > 0, back_second.reshape(HEIGHT, WIDTH, C), 0.0).astype(jnp.bfloat16)
    first_rows = first_map.reshape(POSITIONS, C)
    first_wgrad = jnp.dot(input_rows.T, first_rows, preferred_element_type=jnp.float32) * normalizer
    summed = jnp.dot(first_rows, first_weight.T, preferred_element_type=jnp.float32) + grad_rows.astype(jnp.float32)
    input_grad = image_tiles(summed.astype(jnp.bfloat16).reshape(HEIGHT, WIDTH, C))
    return (input_grad, third_wgrad, group_wgrad, first_wgrad)
```

```python
import functools
import math

import jax
import jax.numpy as jnp
from jax import lax
from jax.experimental import pallas as pl
from jax.experimental.pallas import tpu as pltpu
from jax.sharding import PartitionSpec as P

NT = (((1,), (1,)), ((), ()))
NN = (((1,), (0,)), ((), ()))
BF = jnp.bfloat16
F32 = jnp.float32


def dot(a, b, dims=NN):
    return lax.dot_general(a, b, dims, preferred_element_type=F32)


def spread(k, bits):
    return sum(((k >> at) & 1) << bit for at, bit in enumerate(bits))


class Sums:
    def __init__(self, k, acc, column, snd, rcv, last, core, order, out, place):
        self.k, self.acc, self.order, self.out, self.place = k, acc, order, out, place
        self.snd, self.rcv, self.last, self.core = snd, rcv, last, core
        self.cols = snd.shape[-1]
        self.lanes = pl.ds(column, self.cols)
        self.copies = {}

    def rows(self, chip):
        size = 2 * self.k.unit
        return pl.ds(pl.multiple_of(chip * size, size), size)

    def at_core(self, chip, core):
        unit = self.k.unit
        return pl.ds(pl.multiple_of((2 * chip + core) * unit, unit), unit)

    def plan(self, r, other):
        k, order = self.k, self.order
        bits = sorted(order[r + 1 :])
        base = sum(k.bit(b) * (1 << b) for b in order[:r])
        mine = k.bit(order[r])
        base = base + (1 - mine if other else mine) * (1 << order[r])
        offset = k.chips - (1 << (len(order) - r))
        return base, bits, offset

    def send(self, r):
        k = self.k
        base, bits, offset = self.plan(r, True)
        count = 1 << len(bits)
        for i in range(count):
            part = self.acc[self.rows(base + spread(i, bits)), self.lanes]
            self.snd[offset + i] = part.astype(BF).reshape(2, k.unit, self.cols)
        there = k.p ^ (2 << self.order[r])
        if r < len(self.order) - 1:
            span = pl.ds(offset, count)
            self.copies[r] = [k.push(self.snd.at[span], self.rcv.at[span], there)]
        else:
            chip = there // 2
            own, _, _ = self.plan(r, False)
            self.copies[r] = [
                k.push(self.snd.at[offset, j], self.last.at[k.c], 2 * chip + j, pair=j) for j in (0, 1)
            ]
            self.copies["core"] = [
                k.push(self.acc.at[self.at_core(own, 1 - k.c), self.lanes], self.core, k.p ^ 1)
            ]

    def receive(self, r):
        k = self.k
        base, bits, offset = self.plan(r, False)
        if r < len(self.order) - 1:
            self.copies[r][0].wait_recv()
            for i in range(1 << len(bits)):
                rows = self.rows(base + spread(i, bits))
                got = self.rcv[offset + i].reshape(2 * k.unit, self.cols)
                self.acc[rows, self.lanes] += got.astype(F32)
        else:
            k.wait_pair(self.copies[r])
            self.copies["core"][0].wait_recv()
            mine = self.acc[self.at_core(base, k.c), self.lanes] + self.last[k.c].astype(F32)
            theirs = self.core[...] + self.last[1 - k.c].astype(F32)
            at_mine, at_theirs = self.place(k.c), self.place(1 - k.c)
            self.out[:, pl.ds(pl.multiple_of(at_mine, self.cols), self.cols)] = mine
            self.out[:, pl.ds(pl.multiple_of(at_theirs, self.cols), self.cols)] = theirs

    def finish(self):
        for group in self.copies.values():
            for copy in group:
                copy.wait_send()


class Device:
    def __init__(self, chips, unit, sems):
        self.chips, self.unit, self.sems = chips, unit, sems
        self.p = lax.axis_index("space")
        self.c = lax.rem(self.p, 2)
        self.q = self.p // 2
        self.used = 0

    def bit(self, b):
        return lax.rem(self.q // (1 << b), 2)

    def sem(self, count=1):
        self.used += count
        assert self.used <= self.sems.shape[0]
        return self.used - count

    def push(self, src, dst, there, pair=None):
        if pair is None:
            receive = self.sem()
        else:
            if pair == 0:
                self.base = self.sem(2)
            receive = self.base + self.c
        copy = pltpu.make_async_remote_copy(
            src_ref=src,
            dst_ref=dst,
            send_sem=self.sems.at[self.sem()],
            recv_sem=self.sems.at[receive],
            device_id={"space": there},
            device_id_type=pl.DeviceIdType.MESH,
        )
        copy.start()
        if pair == 1:
            copy.base = self.base
        return copy

    def wait_pair(self, copies):
        base = copies[1].base
        for at in (0, 1):
            self.arrival(copies[1].dst_ref, self.sems.at[base + at]).wait_recv()

    def arrival(self, ref, sem):
        return pltpu.make_async_remote_copy(
            src_ref=ref,
            dst_ref=ref,
            send_sem=sem,
            recv_sem=sem,
            device_id={"space": self.p ^ 1},
            device_id_type=pl.DeviceIdType.MESH,
        )

    def fetch(self, src, dst):
        copy = pltpu.make_async_copy(src, dst, self.sems.at[self.sem()])
        copy.start()
        return copy


def kernel(
    chips, normalizer,
    g_ref, x_ref, h2_ref, h1_ref, w3_ref, gw_ref, w1_ref,
    in_ref, third_ref, group_ref, first_ref,
    g, x, h2, h1, w3, gw, w1, inner, shifted, first, other, xt, h1t, dense, taps_t,
    acc_t, acc_f, acc_g, snd_t, rcv_t, last_t, core_t, snd_f, rcv_f, last_f, core_f,
    snd_g, rcv_g, piece_g, last_g, core_g, out_t, out_f, out_g, out_in, sems,
):
    tall, wide, channels = g_ref.shape
    unit = third_ref.shape[0]
    block = h1.shape[-1]
    width = 2 * wide
    size = tall * width
    taps = gw.shape[1]
    gap = taps // 9
    bits = chips.bit_length() - 1
    k = Device(chips, unit, sems)
    p, c, q = k.p, k.c, k.q
    a = k.bit(0)
    has_up, has_down = q > 0, q < chips - 1

    def lanes(j, core):
        return pl.ds(pl.multiple_of((2 * j + core) * block, block), block)

    order = [0, tall - 1] + list(range(1, tall - 1))
    load_w3 = [k.fetch(w3_ref.at[lanes(j, c)], w3.at[j]) for j in (0, 1)]
    load_g, load_h2 = {}, {}
    for y in order:
        load_g[y] = k.fetch(g_ref.at[y], g.at[y, c])
        load_h2[y] = k.fetch(h2_ref.at[y], h2.at[y, c])
    load_gw = [k.fetch(gw_ref.at[:, lanes(j, c)], gw.at[j]) for j in (0, 1)]
    load_x = k.fetch(x_ref, x.at[:, c])
    load_h1 = k.fetch(h1_ref.at[pl.ds(a * tall, tall)], h1.at[a])
    load_w1 = k.fetch(w1_ref, w1)

    barrier = pltpu.get_barrier_semaphore()
    friends = [p ^ 1]
    for b in range(bits):
        friends += [p ^ (2 << b), p ^ (2 << b) ^ 1]
    far = 3 << (bits - 1)
    friends += [p ^ far, p ^ far ^ 1]

    def greet(there):
        pl.semaphore_signal(barrier, inc=1, device_id={"space": there}, device_id_type=pl.DeviceIdType.MESH)

    for there in friends:
        greet(there)
    outer = jnp.where(a == 0, p - 2, p + 2)
    has_outer = jnp.where(a == 0, q > 0, q < chips - 1)

    @pl.when(has_outer)
    def _():
        greet(outer)

    pl.semaphore_wait(barrier, len(friends) + jnp.where(has_outer, 1, 0))

    send_h1 = pltpu.make_async_remote_copy(
        src_ref=h1_ref.at[pl.ds((1 - a) * tall, tall)],
        dst_ref=h1.at[a],
        send_sem=sems.at[k.sem()],
        recv_sem=sems.at[k.sem()],
        device_id={"space": p ^ 2},
        device_id_type=pl.DeviceIdType.MESH,
    )

    @pl.when(a == 0)
    def _():
        send_h1.start()

    core_g_copy, core_h2_copy = {}, {}
    for y in order:
        core_g_copy[y] = k.push(g_ref.at[y], g.at[y, c], p ^ 1)
        core_h2_copy[y] = k.push(h2_ref.at[y], h2.at[y, c], p ^ 1)
    core_x_copy = k.push(x_ref, x.at[:, c], p ^ 1)

    for copy in load_w3:
        copy.wait()

    def inner_row(y):
        load_g[y].wait()
        load_h2[y].wait()
        core_g_copy[y].wait_recv()
        core_h2_copy[y].wait_recv()
        rows = g[y].reshape(width, channels)
        for j in (0, 1):
            back = dot(rows, w3[j], NT)
            mask = h2[y, :, :, lanes(j, c)].reshape(width, block)
            inner[j, y + 1] = jnp.where(mask > 0, back, 0.0).astype(BF)

    inner_row(0)
    inner_row(tall - 1)

    halos = []
    for j in (0, 1):
        for source, target, there, goes, comes in (
            (1, tall + 1, p - 2, has_up, has_down),
            (tall, 0, p + 2, has_down, has_up),
        ):
            copy = pltpu.make_async_remote_copy(
                src_ref=inner.at[j, source],
                dst_ref=inner.at[j, target],
                send_sem=sems.at[k.sem()],
                recv_sem=sems.at[k.sem()],
                device_id={"space": there},
                device_id_type=pl.DeviceIdType.MESH,
            )
            halos.append((j, copy, goes, comes, target))

            @pl.when(goes)
            def _(copy=copy):
                copy.start()

    @pl.when(a == 1)
    def _():
        send_h1.start()

    for y in range(1, tall - 1):
        inner_row(y)

    low = list(range(1, bits)) + [0]
    high = list(range(1, bits))[::-1] + [0]
    cross = [1, 0] + list(range(2, bits))
    plain = list(range(bits))
    del plain

    third = [
        Sums(k, acc_t.at[j], 0, snd_t.at[j], rcv_t.at[j], last_t.at[j], core_t.at[j], route, out_t,
             functools.partial(lambda j, core: (2 * j + core) * block, j))
        for j, route in ((0, low), (1, high))
    ]
    for at in range(0, channels, block):
        left = h2[:, :, :, at : at + block].reshape(size, block).T
        for j in (0, 1):
            right = g[:, :, :, lanes(j, c)].reshape(size, block)
            acc_t[j, at : at + block, :] = dot(left, right) * normalizer
    third[0].send(0)
    third[1].send(0)

    load_x.wait()
    core_x_copy.wait_recv()
    for at in range(0, channels, block):
        xt[at : at + block, :] = x[:, :, :, at : at + block].reshape(size, block).T

    own = (
        lax.broadcasted_iota(jnp.int32, (block, block), 0) // gap
        == lax.broadcasted_iota(jnp.int32, (block, block), 1) // gap
    )
    for j in (0, 1):
        load_gw[j].wait()
        for tap in range(9):
            part = gw[j, tap * gap : (tap + 1) * gap, :].astype(F32)
            full = jnp.concatenate([part] * (block // gap), 0)
            dense[j, tap] = jnp.where(own, full, 0.0).astype(BF)

    column = lax.broadcasted_iota(jnp.int32, (width, block), 0)

    def shift_row(j, y):
        piece = inner[j, y]
        wider = piece.astype(F32)
        before = jnp.where(column == width - 1, 0.0, pltpu.roll(wider, width - 1, 0))
        after = jnp.where(column == 0, 0.0, pltpu.roll(wider, 1, 0))
        at = slice(y * width, (y + 1) * width)
        shifted[j, 0, at, :] = before.astype(BF)
        shifted[j, 1, at, :] = piece
        shifted[j, 2, at, :] = after.astype(BF)

    for j in (0, 1):
        for y in range(1, tall + 1):
            shift_row(j, y)
    taps_t[...] = jnp.zeros_like(taps_t)

    core_first, group_copies = {}, {}
    top = q // (chips // 4)
    below = lax.rem(q, chips // 4)
    low_bits = list(range(bits - 2))

    def group_rows(chip, core=None):
        if core is None:
            return pl.ds(pl.multiple_of(chip * 2 * unit, 2 * unit), 2 * unit)
        return pl.ds(pl.multiple_of((2 * chip + core) * unit, unit), unit)

    def group_send(j, r):
        done, b, rest = low_bits[:r], low_bits[r], low_bits[r + 1 :]
        base = sum(k.bit(d) * (1 << d) for d in done) + (1 - k.bit(b)) * (1 << b)
        offset = chips // 4 - (1 << (len(low_bits) - r))
        count = 1 << len(rest)
        for i in range(count):
            part = acc_g[j, group_rows(base + spread(i, rest)), :]
            snd_g[j, offset + i] = part.astype(BF).reshape(2, unit, taps)
        span = pl.ds(offset, count)
        group_copies[j, r] = k.push(snd_g.at[j, span], rcv_g.at[j, span], p ^ (2 << b))

    def group_receive(j, r):
        done, b, rest = low_bits[:r], low_bits[r], low_bits[r + 1 :]
        base = sum(k.bit(d) * (1 << d) for d in done) + k.bit(b) * (1 << b)
        offset = chips // 4 - (1 << (len(low_bits) - r))
        group_copies[j, r].wait_recv()
        for i in range(1 << len(rest)):
            got = rcv_g[j, offset + i].reshape(2 * unit, taps).astype(F32)
            acc_g[j, group_rows(base + spread(i, rest)), :] += got

    group_base = k.sem(4)
    group_core = (k.sem(), k.sem())
    group_last = {}

    def group_final(j):
        owner = 2 * j + c
        piece_g[j] = acc_g[j, group_rows(below), :].astype(BF).reshape(2, unit, taps)
        copies = []
        for core in (0, 1):
            copies.append(
                pltpu.make_async_remote_copy(
                    src_ref=piece_g.at[j, core],
                    dst_ref=last_g.at[top],
                    send_sem=sems.at[k.sem()],
                    recv_sem=sems.at[group_base + top],
                    device_id={"space": 2 * (owner * (chips // 4) + below) + core},
                    device_id_type=pl.DeviceIdType.MESH,
                )
            )
        across = pltpu.make_async_remote_copy(
            src_ref=acc_g.at[j, group_rows(below, 1 - c)],
            dst_ref=core_g,
            send_sem=sems.at[group_core[0]],
            recv_sem=sems.at[group_core[1]],
            device_id={"space": p ^ 1},
            device_id_type=pl.DeviceIdType.MESH,
        )
        group_last[j] = (copies, across)

        @pl.when(owner == top)
        def _():
            across.start()

        @pl.when(owner != top)
        def _():
            for copy in copies:
                copy.start()

    def conv(j):
        for i, copy, _, comes, target in halos:
            if i == j:

                @pl.when(comes)
                def _(copy=copy):
                    copy.wait_recv()

                @pl.when(jnp.logical_not(comes))
                def _(target=target):
                    inner[j, target] = jnp.zeros((width, block), BF)

        @pl.when(a == j)
        def _():
            load_h1.wait()

        @pl.when(a != j)
        def _():
            send_h1.wait_recv()

        shift_row(j, 0)
        shift_row(j, tall + 1)

        @pl.loop(0, tall)
        def _(y):
            total = None
            for tap in range(9):
                u, v = tap // 3 - 1, tap % 3 - 1
                rows = pl.ds(pl.multiple_of((y + 1 - u) * width, width), width)
                term = dot(shifted[j, v + 1, rows, :], dense[j, tap], NT)
                total = term if total is None else total + term
            result = jnp.where(h1[j, y] > 0, total, 0.0).astype(BF)
            first[j, y] = result.reshape(2, wide, block)

        core_first[j] = k.push(first.at[j, :, 1 - c], other.at[j], p ^ 1)

        for y in range(tall):
            h1t[:, y * width : (y + 1) * width] = h1[j, y].T
        for tap in range(9):
            u, v = tap // 3 - 1, tap % 3 - 1
            at = (1 - u) * width
            term = dot(h1t[...], shifted[j, v + 1, at : at + size, :])
            term = jnp.where(own, term, 0.0)
            folded = term[:gap]
            for i in range(1, block // gap):
                folded = folded + term[i * gap : (i + 1) * gap]
            taps_t[tap * gap : (tap + 1) * gap, :] = folded * normalizer
        acc_g[j] = taps_t[...].T[:, :taps]
        if low_bits:
            group_send(j, 0)

        for at in range(0, channels, block):
            right = first[j].reshape(size, block)
            acc_f[j, at : at + block, :] = dot(xt[at : at + block, :], right) * normalizer

    half = block // 2

    def first_sums(j, h, route):
        i = 2 * j + h
        return Sums(k, acc_f.at[j], h * half, snd_f.at[i], rcv_f.at[i], last_f.at[i], core_f.at[i], route, out_f,
                    functools.partial(lambda j, h, core: (2 * j + core) * block + h * half, j, h))

    conv(0)
    early = [first_sums(0, 0, low), first_sums(0, 1, high)]
    for piece in early:
        piece.send(0)
    for piece in third:
        piece.receive(0)
        piece.send(1)

    conv(1)
    late = [first_sums(1, 0, [0] + list(range(1, bits))), first_sums(1, 1, cross)]
    for piece in late:
        piece.send(0)
    for r in range(len(low_bits)):
        for j in (0, 1):
            group_receive(j, r)
            if r + 1 < len(low_bits):
                group_send(j, r + 1)
    for j in (0, 1):
        group_final(j)

    for r in range(1, bits):
        for piece in third if r > 1 else []:
            piece.receive(r - 1)
            piece.send(r)
        for piece in early + late:
            piece.receive(r - 1)
            piece.send(r)
        if r == 1:
            load_w1.wait()
            total = g[:, c].reshape(tall * wide, channels).astype(F32)
            for j in (0, 1):
                core_first[j].wait_recv()
                total = total + dot(first[j, :, c].reshape(tall * wide, block), w1[:, lanes(j, c)], NT)
                total = total + dot(other[j].reshape(tall * wide, block), w1[:, lanes(j, 1 - c)], NT)
            out_in[...] = total.astype(BF).reshape(tall, wide, channels)
            store_in = k.fetch(out_in, in_ref)
    for piece in third:
        piece.receive(bits - 1)
    store_third = k.fetch(out_t, third_ref)

    for t in range(4):

        @pl.when(top != t)
        def _(t=t):
            k.arrival(last_g.at[t], sems.at[group_base + t]).wait_recv()

    holder = lax.rem(top, 2)

    @pl.when(holder == c)
    def _():
        out_g[...] = acc_g[top // 2, group_rows(below, c), :]

    @pl.when(holder != c)
    def _():
        k.arrival(core_g, sems.at[group_core[1]]).wait_recv()
        out_g[...] = core_g[...]

    for t in range(4):

        @pl.when(top != t)
        def _(t=t):
            out_g[...] += last_g[t].astype(F32)

    store_group = k.fetch(out_g, group_ref)
    for piece in early + late:
        piece.receive(bits - 1)
    store_first = k.fetch(out_f, first_ref)

    for y in order:
        core_g_copy[y].wait_send()
        core_h2_copy[y].wait_send()
    core_x_copy.wait_send()
    send_h1.wait_send()
    for _, copy, goes, _, _ in halos:

        @pl.when(goes)
        def _(copy=copy):
            copy.wait_send()

    for j in (0, 1):
        core_first[j].wait_send()
        copies, across = group_last[j]

        @pl.when(2 * j + c == top)
        def _(across=across):
            across.wait_send()

        @pl.when(2 * j + c != top)
        def _(copies=copies):
            for copy in copies:
                copy.wait_send()

    for copy in group_copies.values():
        copy.wait_send()
    for piece in third + early + late:
        piece.finish()
    for copy in (store_in, store_third, store_group, store_first):
        copy.wait()


def per_device(
    outer_grad, block_input, third_input, second_input, third_weight, group_weight, first_weight
):
    devices = lax.axis_size("space")
    chips = devices // 2
    _, tall, wide, channels = outer_grad.shape
    block = second_input.shape[3]
    taps = group_weight.shape[1]
    unit = channels // devices
    width, size = 2 * wide, 2 * tall * wide
    half = block // 2
    normalizer = 1.0 / math.sqrt(tall * wide * devices)
    padded = -(-taps // 128) * 128
    anywhere = pl.BlockSpec(memory_space=pl.ANY)

    def vmem(*shape, dtype=BF):
        return pltpu.VMEM(shape, dtype)

    scratch = [
        vmem(tall, 2, wide, channels),
        vmem(tall, 2, wide, channels),
        vmem(tall, 2, wide, channels),
        vmem(2, tall, width, block),
        vmem(2, block, channels),
        vmem(2, taps, block),
        vmem(channels, channels),
        vmem(2, tall + 2, width, block),
        vmem(2, 3, (tall + 2) * width, block),
        vmem(2, tall, 2, wide, block),
        vmem(2, tall, wide, block),
        vmem(channels, size),
        vmem(block, size),
        vmem(2, 9, block, block),
        vmem(padded, block, dtype=F32),
        vmem(2, channels, block, dtype=F32),
        vmem(2, channels, block, dtype=F32),
        vmem(2, block, taps, dtype=F32),
        vmem(2, chips, 2, unit, block),
        vmem(2, chips, 2, unit, block),
        vmem(2, 2, unit, block),
        vmem(2, unit, block, dtype=F32),
        vmem(4, chips, 2, unit, half),
        vmem(4, chips, 2, unit, half),
        vmem(4, 2, unit, half),
        vmem(4, unit, half, dtype=F32),
        vmem(2, max(chips // 4, 1), 2, unit, taps),
        vmem(2, max(chips // 4, 1), 2, unit, taps),
        vmem(2, 2, unit, taps),
        vmem(4, unit, taps),
        vmem(unit, taps, dtype=F32),
        vmem(unit, channels, dtype=F32),
        vmem(unit, channels, dtype=F32),
        vmem(unit, taps, dtype=F32),
        vmem(tall, wide, channels),
        pltpu.SemaphoreType.DMA((256,)),
    ]
    input_grad, third_wgrad, group_wgrad, first_wgrad = pl.pallas_call(
        functools.partial(kernel, chips, normalizer),
        in_specs=[anywhere] * 7,
        out_specs=[anywhere] * 4,
        out_shape=[
            jax.ShapeDtypeStruct((tall, wide, channels), BF),
            jax.ShapeDtypeStruct((unit, channels), F32),
            jax.ShapeDtypeStruct((unit, taps), F32),
            jax.ShapeDtypeStruct((unit, channels), F32),
        ],
        scratch_shapes=scratch,
        compiler_params=pltpu.CompilerParams(
            collective_id=0, has_side_effects=True, vmem_limit_bytes=56 * 2**20
        ),
        cost_estimate=pl.CostEstimate(
            flops=9 * 10**9, bytes_accessed=12 * 2**20, transcendentals=0
        ),
    )(
        outer_grad[0],
        block_input[0],
        third_input[0],
        second_input[0],
        third_weight,
        group_weight.T,
        first_weight,
    )
    return input_grad[None], third_wgrad, group_wgrad, first_wgrad


def solution(mesh):
    spread_out = P(("parts", "space"), None, None, None)
    rows = P(("parts", "space"), None)
    return jax.shard_map(
        per_device,
        mesh=mesh,
        in_specs=(spread_out,) * 4 + (P(),) * 3,
        out_specs=(spread_out, rows, rows, rows),
        check_vma=False,
    )
```

```python
import functools
import math

import jax
import jax.numpy as jnp
from jax import lax
from jax.experimental import pallas as pl
from jax.experimental.pallas import tpu as pltpu
from jax.sharding import PartitionSpec as P

NT = (((1,), (1,)), ((), ()))
NN = (((1,), (0,)), ((), ()))
BF = jnp.bfloat16
F32 = jnp.float32


def dot(a, b, dims=NN):
    return lax.dot_general(a, b, dims, preferred_element_type=F32)


def spread(k, bits):
    return sum(((k >> at) & 1) << bit for at, bit in enumerate(bits))


class Link:
    def __init__(self, k, src, dst, there, goes=None, comes=None, receive=None):
        self.goes, self.comes = goes, comes
        self.started = self.gone = False
        self.left_if = None
        self.copy = pltpu.make_async_remote_copy(
            src_ref=src,
            dst_ref=dst,
            send_sem=k.sems.at[k.sem()],
            recv_sem=k.sems.at[k.sem() if receive is None else receive],
            device_id={"space": there},
            device_id_type=pl.DeviceIdType.MESH,
        )
        k.links.append(self)

    def start(self, also=None):
        self.started = True
        run(self.copy.start, self.goes, also)

    def arrive(self):
        run(self.copy.wait_recv, self.comes)

    def leave(self, also=None):
        self.gone = also is None
        self.left_if = also
        run(self.copy.wait_send, self.goes, also)


def run(act, *conditions):
    conditions = [c for c in conditions if c is not None]
    if conditions:
        pl.when(functools.reduce(jnp.logical_and, conditions))(act)
    else:
        act()


class Sums:
    def __init__(self, k, acc, column, snd, rcv, last, core, order, out, place):
        self.k, self.acc, self.order, self.out, self.place = k, acc, order, out, place
        self.snd, self.rcv, self.last, self.core = snd, rcv, last, core
        self.cols = snd.shape[-1]
        self.lanes = pl.ds(column, self.cols)
        self.links = {}
        for r, b in enumerate(order):
            _, bits, offset = self.plan(r, True)
            there = k.p ^ (2 << b)
            if r < len(order) - 1:
                span = pl.ds(offset, 1 << len(bits))
                self.links[r] = [Link(k, snd.at[span], rcv.at[span], there)]
            else:
                own, _, _ = self.plan(r, False)
                base = k.sem(2)
                self.arrivals = [k.arrival(last.at[at], base + at) for at in (0, 1)]
                self.links[r] = [
                    Link(k, snd.at[offset, j], last.at[k.c], 2 * (there // 2) + j, receive=base + k.c)
                    for j in (0, 1)
                ]
                self.across = Link(k, acc.at[self.at_core(own, 1 - k.c), self.lanes], core, k.p ^ 1)

    def rows(self, chip):
        size = 2 * self.k.unit
        return pl.ds(pl.multiple_of(chip * size, size), size)

    def at_core(self, chip, core):
        unit = self.k.unit
        return pl.ds(pl.multiple_of((2 * chip + core) * unit, unit), unit)

    def plan(self, r, other):
        k, order = self.k, self.order
        bits = sorted(order[r + 1 :])
        base = sum(k.bit(b) * (1 << b) for b in order[:r])
        mine = k.bit(order[r])
        base = base + (1 - mine if other else mine) * (1 << order[r])
        offset = k.chips - (1 << (len(order) - r))
        return base, bits, offset

    def send(self, r):
        k = self.k
        base, bits, offset = self.plan(r, True)
        for i in range(1 << len(bits)):
            part = self.acc[self.rows(base + spread(i, bits)), self.lanes]
            self.snd[offset + i] = part.astype(BF).reshape(2, k.unit, self.cols)
        for link in self.links[r]:
            link.start()
        if r == len(self.order) - 1:
            self.across.start()

    def receive(self, r):
        k = self.k
        base, bits, offset = self.plan(r, False)
        if r < len(self.order) - 1:
            self.links[r][0].arrive()
            for i in range(1 << len(bits)):
                rows = self.rows(base + spread(i, bits))
                got = self.rcv[offset + i].reshape(2 * k.unit, self.cols)
                self.acc[rows, self.lanes] += got.astype(F32)
        else:
            for arrival in self.arrivals:
                arrival.wait_recv()
            self.across.arrive()
            mine = self.acc[self.at_core(base, k.c), self.lanes] + self.last[k.c].astype(F32)
            theirs = self.core[...] + self.last[1 - k.c].astype(F32)
            at_mine, at_theirs = self.place(k.c), self.place(1 - k.c)
            self.out[:, pl.ds(pl.multiple_of(at_mine, self.cols), self.cols)] = mine
            self.out[:, pl.ds(pl.multiple_of(at_theirs, self.cols), self.cols)] = theirs

    def step(self, r):
        self.receive(r)
        self.send(r + 1)


class Device:
    def __init__(self, chips, unit, sems):
        self.chips, self.unit, self.sems = chips, unit, sems
        self.p = lax.axis_index("space")
        self.c = lax.rem(self.p, 2)
        self.q = self.p // 2
        self.used = 0
        self.links = []

    def bit(self, b):
        return lax.rem(self.q // (1 << b), 2)

    def sem(self, count=1):
        self.used += count
        assert self.used <= self.sems.shape[0]
        return self.used - count

    def arrival(self, ref, sem):
        return pltpu.make_async_remote_copy(
            src_ref=ref,
            dst_ref=ref,
            send_sem=self.sems.at[sem],
            recv_sem=self.sems.at[sem],
            device_id={"space": self.p ^ 1},
            device_id_type=pl.DeviceIdType.MESH,
        )

    def fetch(self, src, dst):
        copy = pltpu.make_async_copy(src, dst, self.sems.at[self.sem()])
        copy.start()
        return copy

    def finish(self):
        for link in self.links:
            if link.started and not link.gone:
                link.leave(None if link.left_if is None else jnp.logical_not(link.left_if))


def kernel(
    chips, normalizer,
    g_ref, x_ref, h2_ref, h1_ref, w3_ref, gw_ref, w1_ref,
    in_ref, third_ref, group_ref, first_ref,
    g, x, h2, h1, w3, gw, w1, inner, shifted, first, other, xt, h1t, dense, taps_t,
    acc_t, acc_f, acc_g, snd_t, rcv_t, last_t, core_t, snd_f, rcv_f, last_f, core_f,
    snd_g, rcv_g, piece_g, last_g, core_g, out_t, out_f, out_g, out_in, sems,
):
    tall, wide, channels = g_ref.shape
    unit = third_ref.shape[0]
    block = h1.shape[-1]
    half = block // 2
    width = 2 * wide
    size = tall * width
    taps = gw.shape[1]
    gap = taps // 9
    bits = chips.bit_length() - 1
    k = Device(chips, unit, sems)
    p, c, q = k.p, k.c, k.q
    a = k.bit(0)
    even, odd = a == 0, a == 1
    has_up, has_down = q > 0, q < chips - 1

    def lanes(j, core):
        return pl.ds(pl.multiple_of((2 * j + core) * block, block), block)

    order = [0, tall - 1] + list(range(1, tall - 1))
    load_g = {y: k.fetch(g_ref.at[y], g.at[y, c]) for y in order}
    load_w3 = [k.fetch(w3_ref.at[lanes(j, c)], w3.at[j]) for j in (0, 1)]
    load_h2 = {y: k.fetch(h2_ref.at[y], h2.at[y, c]) for y in order}

    barrier = pltpu.get_barrier_semaphore()
    friends = [p ^ 1]
    for b in range(bits):
        friends += [p ^ (2 << b), p ^ (2 << b) ^ 1]
    far = 3 << (bits - 1)
    friends += [p ^ far, p ^ far ^ 1]

    def greet(there):
        pl.semaphore_signal(barrier, inc=1, device_id={"space": there}, device_id_type=pl.DeviceIdType.MESH)

    for there in friends:
        greet(there)
    outer = jnp.where(even, p - 2, p + 2)
    has_outer = jnp.where(even, q > 0, q < chips - 1)
    run(functools.partial(greet, outer), has_outer)

    def inner_tile(rows, tile):
        side = pl.ds(pl.multiple_of(tile * wide, wide), wide)
        left = jnp.concatenate([g[y, tile] for y in rows], 0)
        for j in (0, 1):
            back = dot(left, w3[j], NT)
            for i, y in enumerate(rows):
                mask = h2[y, tile, :, lanes(j, c)]
                part = back[i * wide : (i + 1) * wide]
                inner[j, y + 1, side, :] = jnp.where(mask > 0, part, 0.0).astype(BF)

    for copy in (*load_g.values(), *load_w3, *load_h2.values()):
        copy.wait()
    inner_tile(order, c)
    pl.semaphore_wait(barrier, len(friends) + jnp.where(has_outer, 1, 0))

    cut = tall // 4
    link_h1 = [
        Link(k, h1_ref.at[pl.ds((1 - a) * tall + at, rows)], h1.at[a, pl.ds(at, rows)], p ^ 2)
        for at, rows in ((0, cut), (cut, tall - cut))
    ]
    link_g = {y: Link(k, g_ref.at[y], g.at[y, c], p ^ 1) for y in order}
    link_h2 = {y: Link(k, h2_ref.at[y], h2.at[y, c], p ^ 1) for y in order}
    link_x = Link(k, x_ref, x.at[:, c], p ^ 1)
    def edge(j, source, target, there, goes, comes, tile):
        side = pl.ds(pl.multiple_of(tile * wide, wide), wide)
        return Link(k, inner.at[j, source, side], inner.at[j, target, side], there, goes, comes)

    halos = [
        [
            [
                edge(j, 1, tall + 1, p - 2, has_up, has_down, tile),
                edge(j, tall, 0, p + 2, has_down, has_up, tile),
            ]
            for tile in (c, 1 - c)
        ]
        for j in (0, 1)
    ]

    for y in order[:2]:
        link_g[y].start()
        link_h2[y].start()
    for link in halos[0][0]:
        link.start()
    link_h1[0].start()
    link_h1[1].start(also=even)
    for y in order[2:]:
        link_g[y].start()
        link_h2[y].start()
    for y in order[:2]:
        link_g[y].arrive()
        link_h2[y].arrive()
    inner_tile(order[:2], 1 - c)
    for link in halos[0][1]:
        link.start()
    load_x = k.fetch(x_ref, x.at[:, c])
    link_x.start()
    load_gw = [k.fetch(gw_ref.at[:, lanes(j, c)], gw.at[j]) for j in (0, 1)]
    load_h1 = k.fetch(h1_ref.at[pl.ds(a * tall, tall)], h1.at[a])
    load_w1 = k.fetch(w1_ref, w1)
    for y in order[2:]:
        link_g[y].arrive()
        link_h2[y].arrive()
    inner_tile(order[2:], 1 - c)

    low = list(range(1, bits)) + [0]
    high = list(range(1, bits))[::-1] + [0]
    ahead = list(range(bits))
    cross = [1, 0] + list(range(2, bits))
    behind = [0] + list(range(1, bits))[::-1]
    routes = dict(low=low, high=high, ahead=ahead, cross=cross, behind=behind)

    third = [
        Sums(k, acc_t.at[j], 0, snd_t.at[j], rcv_t.at[j], last_t.at[j], core_t.at[j], route, out_t,
             functools.partial(lambda j, core: (2 * j + core) * block, j))
        for j, route in ((0, low), (1, high))
    ]
    for at in range(0, channels, block):
        left = h2[:, :, :, at : at + block].reshape(size, block).T
        for j in (0, 1):
            right = g[:, :, :, lanes(j, c)].reshape(size, block)
            acc_t[j, at : at + block, :] = dot(left, right) * normalizer
    third[0].send(0)
    third[1].send(0)

    load_x.wait()
    link_x.arrive()
    for at in range(0, channels, block):
        xt[at : at + block, :] = x[:, :, :, at : at + block].reshape(size, block).T

    own = (
        lax.broadcasted_iota(jnp.int32, (block, block), 0) // gap
        == lax.broadcasted_iota(jnp.int32, (block, block), 1) // gap
    )
    for j in (0, 1):
        load_gw[j].wait()
        for tap in range(9):
            part = gw[j, tap * gap : (tap + 1) * gap, :].astype(F32)
            full = jnp.concatenate([part] * (block // gap), 0)
            dense[j, tap] = jnp.where(own, full, 0.0).astype(BF)

    column = lax.broadcasted_iota(jnp.int32, (width, block), 0)

    def shift_row(j, y):
        piece = inner[j, y]
        wider = piece.astype(F32)
        before = jnp.where(column == width - 1, 0.0, pltpu.roll(wider, width - 1, 0))
        after = jnp.where(column == 0, 0.0, pltpu.roll(wider, 1, 0))
        at = slice(y * width, (y + 1) * width)
        shifted[j, 0, at, :] = before.astype(BF)
        shifted[j, 1, at, :] = piece
        shifted[j, 2, at, :] = after.astype(BF)

    for j in (0, 1):
        for y in range(1, tall + 1):
            shift_row(j, y)
    taps_t[...] = jnp.zeros_like(taps_t)

    def first_sums(j, h, route):
        i = 2 * j + h
        return Sums(k, acc_f.at[j], h * half, snd_f.at[i], rcv_f.at[i], last_f.at[i], core_f.at[i], route, out_f,
                    functools.partial(lambda j, h, core: (2 * j + core) * block + h * half, j, h))

    early = [first_sums(0, h, routes[name]) for h, name in enumerate(("low", "ahead"))]
    late = [first_sums(1, h, routes[name]) for h, name in enumerate(("ahead", "cross"))]
    link_first = [Link(k, first.at[j, :, 1 - c], other.at[j], p ^ 1) for j in (0, 1)]

    top = q // (chips // 4)
    below = lax.rem(q, chips // 4)
    low_bits = list(range(bits - 2))

    def group_rows(chip, core=None):
        if core is None:
            return pl.ds(pl.multiple_of(chip * 2 * unit, 2 * unit), 2 * unit)
        return pl.ds(pl.multiple_of((2 * chip + core) * unit, unit), unit)

    def group_plan(r, other):
        b, rest = low_bits[r], low_bits[r + 1 :]
        base = sum(k.bit(d) * (1 << d) for d in low_bits[:r])
        base = base + (1 - k.bit(b) if other else k.bit(b)) * (1 << b)
        return base, rest, chips // 4 - (1 << (len(low_bits) - r))

    link_group = {}
    for j in (0, 1):
        for r, b in enumerate(low_bits):
            _, rest, offset = group_plan(r, True)
            span = pl.ds(offset, 1 << len(rest))
            link_group[j, r] = Link(k, snd_g.at[j, span], rcv_g.at[j, span], p ^ (2 << b))
    group_base = k.sem(4)
    group_arrivals = [k.arrival(last_g.at[t], group_base + t) for t in range(4)]
    group_across_sem = k.sem()
    group_across_arrival = k.arrival(core_g, group_across_sem)
    link_last, link_across = [], []
    for j in (0, 1):
        owner = 2 * j + c
        link_last.append(
            [
                Link(k, piece_g.at[j, core], last_g.at[top], 2 * (owner * (chips // 4) + below) + core,
                     goes=owner != top, receive=group_base + top)
                for core in (0, 1)
            ]
        )
        link_across.append(
            Link(k, acc_g.at[j, group_rows(below, 1 - c)], core_g, p ^ 1, goes=owner == top, receive=group_across_sem)
        )

    def group_send(j, r):
        base, rest, offset = group_plan(r, True)
        for i in range(1 << len(rest)):
            part = acc_g[j, group_rows(base + spread(i, rest)), :]
            snd_g[j, offset + i] = part.astype(BF).reshape(2, unit, taps)
        link_group[j, r].start()

    def group_receive(j, r):
        base, rest, offset = group_plan(r, False)
        link_group[j, r].arrive()
        for i in range(1 << len(rest)):
            got = rcv_g[j, offset + i].reshape(2 * unit, taps).astype(F32)
            acc_g[j, group_rows(base + spread(i, rest)), :] += got

    def group_onward(j):
        for r in range(len(low_bits)):
            group_receive(j, r)
            if r + 1 < len(low_bits):
                group_send(j, r + 1)
        piece_g[j] = acc_g[j, group_rows(below), :].astype(BF).reshape(2, unit, taps)
        for link in (*link_last[j], link_across[j]):
            link.start()

    def conv(j, pieces):
        for links in halos[j]:
            for link in links:
                link.arrive()
        for there, target in ((has_down, tall + 1), (has_up, 0)):

            @pl.when(jnp.logical_not(there))
            def _(target=target):
                inner[j, target] = jnp.zeros((width, block), BF)

        run(load_h1.wait, a == j)
        for link in link_h1:
            run(link.copy.wait_recv, a != j)
        shift_row(j, 0)
        shift_row(j, tall + 1)

        @pl.loop(0, tall)
        def _(y):
            total = None
            for tap in range(9):
                u, v = tap // 3 - 1, tap % 3 - 1
                rows = pl.ds(pl.multiple_of((y + 1 - u) * width, width), width)
                term = dot(shifted[j, v + 1, rows, :], dense[j, tap], NT)
                total = term if total is None else total + term
            result = jnp.where(h1[j, y] > 0, total, 0.0).astype(BF)
            first[j, y] = result.reshape(2, wide, block)

        link_first[j].start()
        for at in range(0, channels, block):
            right = first[j].reshape(size, block)
            acc_f[j, at : at + block, :] = dot(xt[at : at + block, :], right) * normalizer
        for piece in pieces:
            piece.send(0)

    def conv_weights(j):
        for y in range(tall):
            h1t[:, y * width : (y + 1) * width] = h1[j, y].T
        for tap in range(9):
            u, v = tap // 3 - 1, tap % 3 - 1
            at = (1 - u) * width
            term = dot(h1t[...], shifted[j, v + 1, at : at + size, :])
            term = jnp.where(own, term, 0.0)
            folded = term[:gap]
            for i in range(1, block // gap):
                folded = folded + term[i * gap : (i + 1) * gap]
            taps_t[tap * gap : (tap + 1) * gap, :] = folded * normalizer
        acc_g[j] = taps_t[...].T[:, :taps]
        if low_bits:
            group_send(j, 0)

    def input_gradient():
        load_w1.wait()
        total = g[:, c].reshape(tall * wide, channels).astype(F32)
        for j in (0, 1):
            link_first[j].arrive()
            total = total + dot(first[j, :, c].reshape(tall * wide, block), w1[:, lanes(j, c)], NT)
            total = total + dot(other[j].reshape(tall * wide, block), w1[:, lanes(j, 1 - c)], NT)
        out_in[...] = total.astype(BF).reshape(tall, wide, channels)
        return k.fetch(out_in, in_ref)

    def group_end():
        for t in range(4):
            run(group_arrivals[t].wait_recv, top != t)
        holder = lax.rem(top, 2)

        @pl.when(holder == c)
        def _():
            out_g[...] = acc_g[top // 2, group_rows(below, c), :]

        @pl.when(holder != c)
        def _():
            group_across_arrival.wait_recv()
            out_g[...] = core_g[...]

        for t in range(4):

            @pl.when(top != t)
            def _(t=t):
                out_g[...] += last_g[t].astype(F32)

        return k.fetch(out_g, group_ref)

    stores = []
    for link in (*halos[0][0], *halos[0][1]):
        link.leave(also=odd)
    for link in (link_h1[1], *halos[1][0], *halos[1][1]):
        link.start(also=odd)
    for link in link_h1:
        link.leave(also=even)
    for link in (*halos[1][0], *halos[1][1]):
        link.start(also=even)
    conv(0, early)

    for piece in third:
        piece.step(0)
    conv_weights(0)
    conv(1, late)
    for r in range(1, bits):
        for piece in early:
            piece.step(r - 1)
        if r == 1:
            conv_weights(1)
        for piece in third if r < bits - 1 else []:
            piece.step(r)
        for piece in late:
            piece.step(r - 1)
        if r == 1:
            group_onward(0)
            group_onward(1)
    stores.append(input_gradient())

    for piece in third:
        piece.receive(bits - 1)
    stores.append(k.fetch(out_t, third_ref))
    for piece in early + late:
        piece.receive(bits - 1)
    stores.append(k.fetch(out_f, first_ref))
    stores.append(group_end())
    k.finish()
    for copy in stores:
        copy.wait()


def hand_over(*refs):
    sources, targets, held, sems = refs[:4], refs[4:8], refs[8:12], refs[12]
    moves = []
    for source, target, place in zip(sources, targets, held):
        pieces = range(source.shape[0]) if len(source.shape) == 3 else [slice(None)]
        for piece in pieces:
            at = len(moves)
            moves.append(
                (
                    pltpu.make_async_copy(source.at[piece], place.at[piece], sems.at[0, at]),
                    pltpu.make_async_copy(place.at[piece], target.at[piece], sems.at[1, at]),
                )
            )
    for load, _ in moves:
        load.start()
    for load, store in moves:
        load.wait()
        store.start()
    for _, store in moves:
        store.wait()


def per_device(
    outer_grad, block_input, third_input, second_input, third_weight, group_weight, first_weight
):
    devices = lax.axis_size("space")
    chips = devices // 2
    _, tall, wide, channels = outer_grad.shape
    block = second_input.shape[3]
    taps = group_weight.shape[1]
    unit = channels // devices
    width, size = 2 * wide, 2 * tall * wide
    half = block // 2
    normalizer = 1.0 / math.sqrt(tall * wide * devices)
    padded = -(-taps // 128) * 128
    anywhere = pl.BlockSpec(memory_space=pl.ANY)

    def vmem(*shape, dtype=BF):
        return pltpu.VMEM(shape, dtype)

    scratch = [
        vmem(tall, 2, wide, channels),
        vmem(tall, 2, wide, channels),
        vmem(tall, 2, wide, channels),
        vmem(2, tall, width, block),
        vmem(2, block, channels),
        vmem(2, taps, block),
        vmem(channels, channels),
        vmem(2, tall + 2, width, block),
        vmem(2, 3, (tall + 2) * width, block),
        vmem(2, tall, 2, wide, block),
        vmem(2, tall, wide, block),
        vmem(channels, size),
        vmem(block, size),
        vmem(2, 9, block, block),
        vmem(padded, block, dtype=F32),
        vmem(2, channels, block, dtype=F32),
        vmem(2, channels, block, dtype=F32),
        vmem(2, block, taps, dtype=F32),
        vmem(2, chips, 2, unit, block),
        vmem(2, chips, 2, unit, block),
        vmem(2, 2, unit, block),
        vmem(2, unit, block, dtype=F32),
        vmem(4, chips, 2, unit, half),
        vmem(4, chips, 2, unit, half),
        vmem(4, 2, unit, half),
        vmem(4, unit, half, dtype=F32),
        vmem(2, max(chips // 4, 1), 2, unit, taps),
        vmem(2, max(chips // 4, 1), 2, unit, taps),
        vmem(2, 2, unit, taps),
        vmem(4, unit, taps),
        vmem(unit, taps, dtype=F32),
        vmem(unit, channels, dtype=F32),
        vmem(unit, channels, dtype=F32),
        vmem(unit, taps, dtype=F32),
        vmem(tall, wide, channels),
        pltpu.SemaphoreType.DMA((256,)),
    ]
    input_grad, third_wgrad, group_wgrad, first_wgrad = pl.pallas_call(
        functools.partial(kernel, chips, normalizer),
        in_specs=[anywhere] * 7,
        out_specs=[anywhere] * 4,
        out_shape=[
            jax.ShapeDtypeStruct((tall, wide, channels), BF),
            jax.ShapeDtypeStruct((unit, channels), F32),
            jax.ShapeDtypeStruct((unit, taps), F32),
            jax.ShapeDtypeStruct((unit, channels), F32),
        ],
        scratch_shapes=scratch,
        compiler_params=pltpu.CompilerParams(
            collective_id=0, has_side_effects=True, vmem_limit_bytes=56 * 2**20
        ),
        cost_estimate=pl.CostEstimate(
            flops=9 * 10**9, bytes_accessed=12 * 2**20, transcendentals=0
        ),
    )(
        outer_grad[0],
        block_input[0],
        third_input[0],
        second_input[0],
        third_weight,
        group_weight.T,
        first_weight,
    )
    results = (input_grad, third_wgrad, group_wgrad, first_wgrad)
    results = pl.pallas_call(
        hand_over,
        in_specs=[anywhere] * 4,
        out_specs=[anywhere] * 4,
        out_shape=[jax.ShapeDtypeStruct(r.shape, r.dtype) for r in results],
        scratch_shapes=[pltpu.VMEM(r.shape, r.dtype) for r in results] + [pltpu.SemaphoreType.DMA((2, tall + 3))],
    )(*results)
    return results[0][None], results[1], results[2], results[3]


def solution(mesh):
    spread_out = P(("parts", "space"), None, None, None)
    rows = P(("parts", "space"), None)
    return jax.shard_map(
        per_device,
        mesh=mesh,
        in_specs=(spread_out,) * 4 + (P(),) * 3,
        out_specs=(spread_out, rows, rows, rows),
        check_vma=False,
    )
```

```python
import functools
import math

import jax
import jax.numpy as jnp
from jax import lax
from jax.experimental import pallas as pl
from jax.experimental.pallas import tpu as pltpu
from jax.sharding import PartitionSpec as P

NT = (((1,), (1,)), ((), ()))
NN = (((1,), (0,)), ((), ()))
BF = jnp.bfloat16
F32 = jnp.float32


def dot(a, b, dims=NN):
    return lax.dot_general(a, b, dims, preferred_element_type=F32)


def spread(k, bits):
    return sum(((k >> at) & 1) << bit for at, bit in enumerate(bits))


class Link:
    def __init__(self, k, src, dst, there, goes=None, comes=None, receive=None):
        self.goes, self.comes = goes, comes
        self.started = self.gone = False
        self.left_if = None
        self.copy = pltpu.make_async_remote_copy(
            src_ref=src,
            dst_ref=dst,
            send_sem=k.sems.at[k.sem()],
            recv_sem=k.sems.at[k.sem() if receive is None else receive],
            device_id={"space": there},
            device_id_type=pl.DeviceIdType.MESH,
        )
        k.links.append(self)

    def start(self, also=None):
        self.started = True
        run(self.copy.start, self.goes, also)

    def arrive(self):
        run(self.copy.wait_recv, self.comes)

    def leave(self, also=None):
        self.gone = also is None
        self.left_if = also
        run(self.copy.wait_send, self.goes, also)


def run(act, *conditions):
    conditions = [c for c in conditions if c is not None]
    if conditions:
        pl.when(functools.reduce(jnp.logical_and, conditions))(act)
    else:
        act()


class Sums:
    def __init__(self, k, acc, column, snd, rcv, last, core, order, direct, out, place):
        self.rounds, self.now = len(order) - direct, 0
        last_bits = order[self.rounds - 1 :]
        self.masks = [spread(d, last_bits) for d in range(1, 1 << len(last_bits))]
        self.k, self.acc, self.order, self.out, self.place = k, acc, order, out, place
        self.snd, self.rcv, self.last, self.core = snd, rcv, last, core
        self.cols = snd.shape[-1]
        self.lanes = pl.ds(column, self.cols)
        self.links = {}
        for r in range(self.rounds - 1):
            _, bits, offset = self.plan(r, True)
            span = pl.ds(offset, 1 << len(bits))
            self.links[r] = [Link(k, snd.at[span], rcv.at[span], k.p ^ (2 << order[r]))]
        base = k.sem(2 * len(self.masks))
        self.arrivals = [k.arrival(last.at[at], base + at) for at in range(2 * len(self.masks))]
        self.offset = k.chips - (1 << len(last_bits))
        self.links[self.rounds - 1] = [
            Link(k, snd.at[self.offset + d, j], last.at[2 * d + k.c], (k.p ^ (2 * mask)) // 2 * 2 + j,
                 receive=base + 2 * d + k.c)
            for d, mask in enumerate(self.masks)
            for j in (0, 1)
        ]
        self.across = Link(k, acc.at[self.at_core(k.q, 1 - k.c), self.lanes], core, k.p ^ 1)

    def rows(self, chip):
        size = 2 * self.k.unit
        return pl.ds(pl.multiple_of(chip * size, size), size)

    def at_core(self, chip, core):
        unit = self.k.unit
        return pl.ds(pl.multiple_of((2 * chip + core) * unit, unit), unit)

    def plan(self, r, other):
        k, order = self.k, self.order
        bits = sorted(order[r + 1 :])
        base = sum(k.bit(b) * (1 << b) for b in order[:r])
        mine = k.bit(order[r])
        base = base + (1 - mine if other else mine) * (1 << order[r])
        offset = k.chips - (1 << (len(order) - r))
        return base, bits, offset

    def pack(self, slot, chip):
        part = self.acc[self.rows(chip), self.lanes]
        self.snd[slot] = part.astype(BF).reshape(2, self.k.unit, self.cols)

    def send(self):
        r = self.now
        if r < self.rounds - 1:
            base, bits, offset = self.plan(r, True)
            for i in range(1 << len(bits)):
                self.pack(offset + i, base + spread(i, bits))
        else:
            for d, mask in enumerate(self.masks):
                self.pack(self.offset + d, self.k.q ^ mask)
            self.across.start()
        for link in self.links[r]:
            link.start()

    def step(self):
        if self.now == self.rounds - 1:
            return
        k = self.k
        base, bits, offset = self.plan(self.now, False)
        self.links[self.now][0].arrive()
        for i in range(1 << len(bits)):
            rows = self.rows(base + spread(i, bits))
            got = self.rcv[offset + i].reshape(2 * k.unit, self.cols)
            self.acc[rows, self.lanes] += got.astype(F32)
        self.now += 1
        self.send()

    def end(self):
        while self.now < self.rounds - 1:
            self.step()
        k = self.k
        for arrival in self.arrivals:
            arrival.wait_recv()
        self.across.arrive()
        mine, theirs = self.acc[self.at_core(k.q, k.c), self.lanes], self.core[...]
        for d in range(len(self.masks)):
            mine = mine + self.last[2 * d + k.c].astype(F32)
            theirs = theirs + self.last[2 * d + 1 - k.c].astype(F32)
        for core, value in ((k.c, mine), (1 - k.c, theirs)):
            self.out[:, pl.ds(pl.multiple_of(self.place(core), self.cols), self.cols)] = value


class Device:
    def __init__(self, chips, unit, sems):
        self.chips, self.unit, self.sems = chips, unit, sems
        self.p = lax.axis_index("space")
        self.c = lax.rem(self.p, 2)
        self.q = self.p // 2
        self.used = 0
        self.links = []

    def bit(self, b):
        return lax.rem(self.q // (1 << b), 2)

    def sem(self, count=1):
        self.used += count
        assert self.used <= self.sems.shape[0]
        return self.used - count

    def arrival(self, ref, sem):
        return pltpu.make_async_remote_copy(
            src_ref=ref,
            dst_ref=ref,
            send_sem=self.sems.at[sem],
            recv_sem=self.sems.at[sem],
            device_id={"space": self.p ^ 1},
            device_id_type=pl.DeviceIdType.MESH,
        )

    def fetch(self, src, dst):
        copy = pltpu.make_async_copy(src, dst, self.sems.at[self.sem()])
        copy.start()
        return copy

    def finish(self):
        for link in self.links:
            if link.started and not link.gone:
                link.leave(None if link.left_if is None else jnp.logical_not(link.left_if))


def kernel(
    chips, normalizer,
    g_ref, x_ref, h2_ref, h1_ref, w3_ref, gw_ref, w1_ref,
    in_ref, third_ref, group_ref, first_ref,
    g, x, h2, h1, w3, gw, w1, inner, shifted, first, other, xt, h1t, dense, taps_t,
    acc_t, acc_f, acc_g, snd_t, rcv_t, last_t, core_t, snd_f, rcv_f, last_f, core_f,
    snd_g, rcv_g, piece_g, last_g, core_g, out_t, out_f, out_g, out_in, sems,
):
    tall, wide, channels = g_ref.shape
    unit = third_ref.shape[0]
    block = h1.shape[-1]
    half = block // 2
    width = 2 * wide
    size = tall * width
    taps = gw.shape[1]
    gap = taps // 9
    bits = chips.bit_length() - 1
    k = Device(chips, unit, sems)
    p, c, q = k.p, k.c, k.q
    a = k.bit(0)
    even, odd = a == 0, a == 1
    has_up, has_down = q > 0, q < chips - 1

    def lanes(j, core):
        return pl.ds(pl.multiple_of((2 * j + core) * block, block), block)

    order = [0, tall - 1] + list(range(1, tall - 1))
    load_g = {y: k.fetch(g_ref.at[y], g.at[y, c]) for y in order}
    load_w3 = [k.fetch(w3_ref.at[lanes(j, c)], w3.at[j]) for j in (0, 1)]
    load_h2 = {y: k.fetch(h2_ref.at[y], h2.at[y, c]) for y in order}

    barrier = pltpu.get_barrier_semaphore()
    friends = [p ^ 1]
    for b in range(bits):
        friends += [p ^ (2 << b), p ^ (2 << b) ^ 1]
    far = 3 << (bits - 1)
    friends += [p ^ far, p ^ far ^ 1]

    def greet(there):
        pl.semaphore_signal(barrier, inc=1, device_id={"space": there}, device_id_type=pl.DeviceIdType.MESH)

    for there in friends:
        greet(there)
    outer = jnp.where(even, p - 2, p + 2)
    has_outer = jnp.where(even, q > 0, q < chips - 1)
    run(functools.partial(greet, outer), has_outer)

    def inner_tile(rows, tile):
        side = pl.ds(pl.multiple_of(tile * wide, wide), wide)
        left = jnp.concatenate([g[y, tile] for y in rows], 0)
        for j in (0, 1):
            back = dot(left, w3[j], NT)
            for i, y in enumerate(rows):
                mask = h2[y, tile, :, lanes(j, c)]
                part = back[i * wide : (i + 1) * wide]
                inner[j, y + 1, side, :] = jnp.where(mask > 0, part, 0.0).astype(BF)

    pl.semaphore_wait(barrier, len(friends) + jnp.where(has_outer, 1, 0))

    link_h1 = [
        Link(k, h1_ref.at[pl.ds((1 - a) * tall + at, rows)], h1.at[a, pl.ds(at, rows)], p ^ 2)
        for at, rows in ((1, tall - 2), (0, 1), (tall - 1, 1))
    ]
    link_g = {y: Link(k, g_ref.at[y], g.at[y, c], p ^ 1) for y in order}
    link_h2 = {y: Link(k, h2_ref.at[y], h2.at[y, c], p ^ 1) for y in order}
    link_x = Link(k, x_ref, x.at[:, c], p ^ 1)
    def edge(j, source, target, there, goes, comes, tile):
        side = pl.ds(pl.multiple_of(tile * wide, wide), wide)
        return Link(k, inner.at[j, source, side], inner.at[j, target, side], there, goes, comes)

    halos = [
        [
            [
                edge(j, 1, tall + 1, p - 2, has_up, has_down, tile),
                edge(j, tall, 0, p + 2, has_down, has_up, tile),
            ]
            for tile in (c, 1 - c)
        ]
        for j in (0, 1)
    ]

    for y in order[:2]:
        link_g[y].start()
        link_h2[y].start()
    link_h1[0].start()
    for y in order[2:]:
        link_g[y].start()
        link_h2[y].start()
    for copy in load_w3:
        copy.wait()
    for y in order[:2]:
        load_g[y].wait()
        load_h2[y].wait()
    inner_tile(order[:2], c)
    for link in halos[0][0]:
        link.start()
    for y in order[:2]:
        link_g[y].arrive()
        link_h2[y].arrive()
    inner_tile(order[:2], 1 - c)
    for link in halos[0][1]:
        link.start()
    load_x = k.fetch(x_ref, x.at[:, c])
    link_x.start()
    load_gw = [k.fetch(gw_ref.at[:, lanes(j, c)], gw.at[j]) for j in (0, 1)]
    load_h1 = k.fetch(h1_ref.at[pl.ds(a * tall, tall)], h1.at[a])
    load_w1 = k.fetch(w1_ref, w1)
    for y in order[2:]:
        load_g[y].wait()
        load_h2[y].wait()
    inner_tile(order[2:], c)
    for y in order[2:]:
        link_g[y].arrive()
        link_h2[y].arrive()
    inner_tile(order[2:], 1 - c)

    low = list(range(1, bits)) + [0]
    high = list(range(1, bits))[::-1] + [0]
    early_routes = ((low, False), (list(range(bits)), True))
    late_routes = ((list(range(bits)), True), (list(range(bits)), True))

    third = [
        Sums(k, acc_t.at[j], 0, snd_t.at[j], rcv_t.at[j], last_t.at[j], core_t.at[j], route, False, out_t,
             functools.partial(lambda j, core: (2 * j + core) * block, j))
        for j, route in ((0, low), (1, high))
    ]
    for at in range(0, channels, block):
        left = h2[:, :, :, at : at + block].reshape(size, block).T
        for j in (0, 1):
            right = g[:, :, :, lanes(j, c)].reshape(size, block)
            acc_t[j, at : at + block, :] = dot(left, right) * normalizer
    third[0].send()
    third[1].send()

    load_x.wait()
    link_x.arrive()
    for at in range(0, channels, block):
        xt[at : at + block, :] = x[:, :, :, at : at + block].reshape(size, block).T

    own = (
        lax.broadcasted_iota(jnp.int32, (block, block), 0) // gap
        == lax.broadcasted_iota(jnp.int32, (block, block), 1) // gap
    )
    for j in (0, 1):
        load_gw[j].wait()
        for tap in range(9):
            part = gw[j, tap * gap : (tap + 1) * gap, :].astype(F32)
            full = jnp.concatenate([part] * (block // gap), 0)
            dense[j, tap] = jnp.where(own, full, 0.0).astype(BF)

    column = lax.broadcasted_iota(jnp.int32, (width, block), 0)

    def shift_row(j, y):
        piece = inner[j, y]
        wider = piece.astype(F32)
        before = jnp.where(column == width - 1, 0.0, pltpu.roll(wider, width - 1, 0))
        after = jnp.where(column == 0, 0.0, pltpu.roll(wider, 1, 0))
        at = slice(y * width, (y + 1) * width)
        shifted[j, 0, at, :] = before.astype(BF)
        shifted[j, 1, at, :] = piece
        shifted[j, 2, at, :] = after.astype(BF)

    for j in (0, 1):
        for y in range(1, tall + 1):
            shift_row(j, y)
    taps_t[...] = jnp.zeros_like(taps_t)

    def first_sums(j, h, route):
        i = 2 * j + h
        return Sums(k, acc_f.at[j], h * half, snd_f.at[i], rcv_f.at[i], last_f.at[i], core_f.at[i], *route, out_f,
                    functools.partial(lambda j, h, core: (2 * j + core) * block + h * half, j, h))

    early = [first_sums(0, h, route) for h, route in enumerate(early_routes)]
    late = [first_sums(1, h, route) for h, route in enumerate(late_routes)]
    link_first = [Link(k, first.at[j, :, 1 - c], other.at[j], p ^ 1) for j in (0, 1)]

    top = q // (chips // 4)
    below = lax.rem(q, chips // 4)
    low_bits = list(range(bits - 2))

    def group_rows(chip, core=None):
        if core is None:
            return pl.ds(pl.multiple_of(chip * 2 * unit, 2 * unit), 2 * unit)
        return pl.ds(pl.multiple_of((2 * chip + core) * unit, unit), unit)

    def group_plan(r, other):
        b, rest = low_bits[r], low_bits[r + 1 :]
        base = sum(k.bit(d) * (1 << d) for d in low_bits[:r])
        base = base + (1 - k.bit(b) if other else k.bit(b)) * (1 << b)
        return base, rest, chips // 4 - (1 << (len(low_bits) - r))

    link_group = {}
    for j in (0, 1):
        for r, b in enumerate(low_bits):
            _, rest, offset = group_plan(r, True)
            span = pl.ds(offset, 1 << len(rest))
            link_group[j, r] = Link(k, snd_g.at[j, span], rcv_g.at[j, span], p ^ (2 << b))
    group_base = k.sem(4)
    group_arrivals = [k.arrival(last_g.at[t], group_base + t) for t in range(4)]
    group_across_sem = k.sem()
    group_across_arrival = k.arrival(core_g, group_across_sem)
    link_last, link_across = [], []
    for j in (0, 1):
        owner = 2 * j + c
        link_last.append(
            [
                Link(k, piece_g.at[j, core], last_g.at[top], 2 * (owner * (chips // 4) + below) + core,
                     goes=owner != top, receive=group_base + top)
                for core in (0, 1)
            ]
        )
        link_across.append(
            Link(k, acc_g.at[j, group_rows(below, 1 - c)], core_g, p ^ 1, goes=owner == top, receive=group_across_sem)
        )

    def group_send(j, r):
        base, rest, offset = group_plan(r, True)
        for i in range(1 << len(rest)):
            part = acc_g[j, group_rows(base + spread(i, rest)), :]
            snd_g[j, offset + i] = part.astype(BF).reshape(2, unit, taps)
        link_group[j, r].start()

    def group_receive(j, r):
        base, rest, offset = group_plan(r, False)
        link_group[j, r].arrive()
        for i in range(1 << len(rest)):
            got = rcv_g[j, offset + i].reshape(2 * unit, taps).astype(F32)
            acc_g[j, group_rows(base + spread(i, rest)), :] += got

    def group_onward(j):
        for r in range(len(low_bits)):
            group_receive(j, r)
            if r + 1 < len(low_bits):
                group_send(j, r + 1)
        piece_g[j] = acc_g[j, group_rows(below), :].astype(BF).reshape(2, unit, taps)
        for link in (*link_last[j], link_across[j]):
            link.start()

    def conv_row(j, y):
        total = None
        for tap in range(9):
            u, v = tap // 3 - 1, tap % 3 - 1
            rows = (y + 1 - u) * width
            rows = pl.ds(rows if isinstance(y, int) else pl.multiple_of(rows, width), width)
            term = dot(shifted[j, v + 1, rows, :], dense[j, tap], NT)
            total = term if total is None else total + term
        result = jnp.where(h1[j, y] > 0, total, 0.0).astype(BF)
        first[j, y] = result.reshape(2, wide, block)

    def conv_inside(j):
        run(load_h1.wait, a == j)
        run(link_h1[0].copy.wait_recv, a != j)

        @pl.loop(1, tall - 1)
        def _(y):
            conv_row(j, y)

        for at in range(0, channels, block):
            right = first[j, 1 : tall - 1].reshape(size - 2 * width, block)
            left = xt[at : at + block, width : size - width]
            acc_f[j, at : at + block, :] = dot(left, right) * normalizer

    def conv_edges(j, pieces):
        for links in halos[j]:
            for link in links:
                link.arrive()
        for there, target in ((has_down, tall + 1), (has_up, 0)):

            @pl.when(jnp.logical_not(there))
            def _(target=target):
                inner[j, target] = jnp.zeros((width, block), BF)

        for link in link_h1[1:]:
            run(link.copy.wait_recv, a != j)
        shift_row(j, 0)
        shift_row(j, tall + 1)
        for y in (0, tall - 1):
            conv_row(j, y)
        for at in range(0, channels, block):
            term = None
            for y in (0, tall - 1):
                left = xt[at : at + block, y * width : (y + 1) * width]
                part = dot(left, first[j, y].reshape(width, block))
                term = part if term is None else term + part
            acc_f[j, at : at + block, :] += term * normalizer
        for piece in pieces:
            piece.send()
        link_first[j].start()

    def conv_weights(j):
        for y in range(tall):
            h1t[:, y * width : (y + 1) * width] = h1[j, y].T
        for tap in range(9):
            u, v = tap // 3 - 1, tap % 3 - 1
            at = (1 - u) * width
            term = dot(h1t[...], shifted[j, v + 1, at : at + size, :])
            term = jnp.where(own, term, 0.0)
            folded = term[:gap]
            for i in range(1, block // gap):
                folded = folded + term[i * gap : (i + 1) * gap]
            taps_t[tap * gap : (tap + 1) * gap, :] = folded * normalizer
        acc_g[j] = taps_t[...].T[:, :taps]
        if low_bits:
            group_send(j, 0)

    def input_gradient():
        load_w1.wait()
        total = g[:, c].reshape(tall * wide, channels).astype(F32)
        for j in (0, 1):
            link_first[j].arrive()
            total = total + dot(first[j, :, c].reshape(tall * wide, block), w1[:, lanes(j, c)], NT)
            total = total + dot(other[j].reshape(tall * wide, block), w1[:, lanes(j, 1 - c)], NT)
        out_in[...] = total.astype(BF).reshape(tall, wide, channels)
        return k.fetch(out_in, in_ref)

    def group_end():
        for t in range(4):
            run(group_arrivals[t].wait_recv, top != t)
        holder = lax.rem(top, 2)

        @pl.when(holder == c)
        def _():
            out_g[...] = acc_g[top // 2, group_rows(below, c), :]

        @pl.when(holder != c)
        def _():
            group_across_arrival.wait_recv()
            out_g[...] = core_g[...]

        for t in range(4):

            @pl.when(top != t)
            def _(t=t):
                out_g[...] += last_g[t].astype(F32)

        return k.fetch(out_g, group_ref)

    stores = []
    for link in (*halos[0][0], *halos[0][1]):
        link.leave(also=odd)
    for link in (*halos[1][0], *halos[1][1], *link_h1[1:]):
        link.start(also=odd)
    link_h1[0].leave(also=even)
    for link in link_h1[1:]:
        link.start(also=even)
    conv_inside(1)
    conv_inside(0)
    conv_edges(0, early)
    for link in link_h1[1:]:
        link.leave(also=even)
    for link in (*halos[1][0], *halos[1][1]):
        link.start(also=even)

    for piece in third:
        piece.step()
    conv_weights(0)
    conv_edges(1, late)
    for piece in early:
        piece.step()
    conv_weights(1)
    for r in range(1, bits):
        for piece in late + third + early:
            piece.step()
        if r == 1:
            group_onward(0)
            group_onward(1)
    stores.append(input_gradient())

    for piece in third:
        piece.end()
    stores.append(k.fetch(out_t, third_ref))
    for piece in early + late:
        piece.end()
    stores.append(k.fetch(out_f, first_ref))
    stores.append(group_end())
    k.finish()
    for copy in stores:
        copy.wait()


def hand_over(*refs):
    sources, targets, held, sems = refs[:4], refs[4:8], refs[8:12], refs[12]
    moves = []
    for source, target, place in zip(sources, targets, held):
        pieces = range(source.shape[0]) if len(source.shape) == 3 else [slice(None)]
        for piece in pieces:
            at = len(moves)
            moves.append(
                (
                    pltpu.make_async_copy(source.at[piece], place.at[piece], sems.at[0, at]),
                    pltpu.make_async_copy(place.at[piece], target.at[piece], sems.at[1, at]),
                )
            )
    for load, _ in moves:
        load.start()
    for load, store in moves:
        load.wait()
        store.start()
    for _, store in moves:
        store.wait()


def per_device(
    outer_grad, block_input, third_input, second_input, third_weight, group_weight, first_weight
):
    devices = lax.axis_size("space")
    chips = devices // 2
    _, tall, wide, channels = outer_grad.shape
    block = second_input.shape[3]
    taps = group_weight.shape[1]
    unit = channels // devices
    width, size = 2 * wide, 2 * tall * wide
    half = block // 2
    normalizer = 1.0 / math.sqrt(tall * wide * devices)
    padded = -(-taps // 128) * 128
    anywhere = pl.BlockSpec(memory_space=pl.ANY)

    def vmem(*shape, dtype=BF):
        return pltpu.VMEM(shape, dtype)

    scratch = [
        vmem(tall, 2, wide, channels),
        vmem(tall, 2, wide, channels),
        vmem(tall, 2, wide, channels),
        vmem(2, tall, width, block),
        vmem(2, block, channels),
        vmem(2, taps, block),
        vmem(channels, channels),
        vmem(2, tall + 2, width, block),
        vmem(2, 3, (tall + 2) * width, block),
        vmem(2, tall, 2, wide, block),
        vmem(2, tall, wide, block),
        vmem(channels, size),
        vmem(block, size),
        vmem(2, 9, block, block),
        vmem(padded, block, dtype=F32),
        vmem(2, channels, block, dtype=F32),
        vmem(2, channels, block, dtype=F32),
        vmem(2, block, taps, dtype=F32),
        vmem(2, chips, 2, unit, block),
        vmem(2, chips, 2, unit, block),
        vmem(2, 2, unit, block),
        vmem(2, unit, block, dtype=F32),
        vmem(4, chips, 2, unit, half),
        vmem(4, chips, 2, unit, half),
        vmem(4, 6, unit, half),
        vmem(4, unit, half, dtype=F32),
        vmem(2, max(chips // 4, 1), 2, unit, taps),
        vmem(2, max(chips // 4, 1), 2, unit, taps),
        vmem(2, 2, unit, taps),
        vmem(4, unit, taps),
        vmem(unit, taps, dtype=F32),
        vmem(unit, channels, dtype=F32),
        vmem(unit, channels, dtype=F32),
        vmem(unit, taps, dtype=F32),
        vmem(tall, wide, channels),
        pltpu.SemaphoreType.DMA((256,)),
    ]
    input_grad, third_wgrad, group_wgrad, first_wgrad = pl.pallas_call(
        functools.partial(kernel, chips, normalizer),
        in_specs=[anywhere] * 7,
        out_specs=[anywhere] * 4,
        out_shape=[
            jax.ShapeDtypeStruct((tall, wide, channels), BF),
            jax.ShapeDtypeStruct((unit, channels), F32),
            jax.ShapeDtypeStruct((unit, taps), F32),
            jax.ShapeDtypeStruct((unit, channels), F32),
        ],
        scratch_shapes=scratch,
        compiler_params=pltpu.CompilerParams(
            collective_id=0, has_side_effects=True, vmem_limit_bytes=56 * 2**20
        ),
        cost_estimate=pl.CostEstimate(
            flops=9 * 10**9, bytes_accessed=12 * 2**20, transcendentals=0
        ),
    )(
        outer_grad[0],
        block_input[0],
        third_input[0],
        second_input[0],
        third_weight,
        group_weight.T,
        first_weight,
    )
    results = (input_grad, third_wgrad, group_wgrad, first_wgrad)
    results = pl.pallas_call(
        hand_over,
        in_specs=[anywhere] * 4,
        out_specs=[anywhere] * 4,
        out_shape=[jax.ShapeDtypeStruct(r.shape, r.dtype) for r in results],
        scratch_shapes=[pltpu.VMEM(r.shape, r.dtype) for r in results] + [pltpu.SemaphoreType.DMA((2, tall + 3))],
    )(*results)
    return results[0][None], results[1], results[2], results[3]


def solution(mesh):
    spread_out = P(("parts", "space"), None, None, None)
    rows = P(("parts", "space"), None)
    return jax.shard_map(
        per_device,
        mesh=mesh,
        in_specs=(spread_out,) * 4 + (P(),) * 3,
        out_specs=(spread_out, rows, rows, rows),
        check_vma=False,
    )
```

```python
import functools
import math

import jax
import jax.numpy as jnp
from jax import lax
from jax.experimental import pallas as pl
from jax.experimental.pallas import tpu as pltpu
from jax.sharding import PartitionSpec as P

NT = (((1,), (1,)), ((), ()))
NN = (((1,), (0,)), ((), ()))
BF = jnp.bfloat16
F32 = jnp.float32


def dot(a, b, dims=NN):
    return lax.dot_general(a, b, dims, preferred_element_type=F32)


def spread(k, bits):
    return sum(((k >> at) & 1) << bit for at, bit in enumerate(bits))


class Link:
    def __init__(self, k, src, dst, there, goes=None, comes=None, receive=None):
        self.goes, self.comes = goes, comes
        self.started = self.gone = False
        self.left_if = None
        self.copy = pltpu.make_async_remote_copy(
            src_ref=src,
            dst_ref=dst,
            send_sem=k.sems.at[k.sem()],
            recv_sem=k.sems.at[k.sem() if receive is None else receive],
            device_id={"space": there},
            device_id_type=pl.DeviceIdType.MESH,
        )
        k.links.append(self)

    def start(self, also=None):
        self.started = True
        run(self.copy.start, self.goes, also)

    def arrive(self):
        run(self.copy.wait_recv, self.comes)

    def leave(self, also=None):
        self.gone = also is None
        self.left_if = also
        run(self.copy.wait_send, self.goes, also)


def run(act, *conditions):
    conditions = [c for c in conditions if c is not None]
    if conditions:
        pl.when(functools.reduce(jnp.logical_and, conditions))(act)
    else:
        act()


class Sums:
    def __init__(self, k, acc, column, snd, rcv, last, core, order, direct, out, place):
        self.rounds, self.now = len(order) - direct, 0
        last_bits = order[self.rounds - 1 :]
        self.masks = [spread(d, last_bits) for d in range(1, 1 << len(last_bits))]
        self.k, self.acc, self.order, self.out, self.place = k, acc, order, out, place
        self.snd, self.rcv, self.last, self.core = snd, rcv, last, core
        self.cols = snd.shape[-1]
        self.lanes = pl.ds(column, self.cols)
        self.links = {}
        for r in range(self.rounds - 1):
            _, bits, offset = self.plan(r, True)
            span = pl.ds(offset, 1 << len(bits))
            self.links[r] = [Link(k, snd.at[span], rcv.at[span], k.p ^ (2 << order[r]))]
        base = k.sem(2 * len(self.masks))
        self.arrivals = [k.arrival(last.at[at], base + at) for at in range(2 * len(self.masks))]
        self.offset = k.chips - (1 << len(last_bits))
        self.links[self.rounds - 1] = [
            Link(k, snd.at[self.offset + d, j], last.at[2 * d + k.c], (k.p ^ (2 * mask)) // 2 * 2 + j,
                 receive=base + 2 * d + k.c)
            for d, mask in enumerate(self.masks)
            for j in (0, 1)
        ]
        self.across = Link(k, acc.at[self.at_core(k.q, 1 - k.c), self.lanes], core, k.p ^ 1)

    def rows(self, chip):
        size = 2 * self.k.unit
        return pl.ds(pl.multiple_of(chip * size, size), size)

    def at_core(self, chip, core):
        unit = self.k.unit
        return pl.ds(pl.multiple_of((2 * chip + core) * unit, unit), unit)

    def plan(self, r, other):
        k, order = self.k, self.order
        bits = sorted(order[r + 1 :])
        base = sum(k.bit(b) * (1 << b) for b in order[:r])
        mine = k.bit(order[r])
        base = base + (1 - mine if other else mine) * (1 << order[r])
        offset = k.chips - (1 << (len(order) - r))
        return base, bits, offset

    def pack(self, slot, chip):
        part = self.acc[self.rows(chip), self.lanes]
        self.snd[slot] = part.astype(BF).reshape(2, self.k.unit, self.cols)

    def send(self):
        r = self.now
        if r < self.rounds - 1:
            base, bits, offset = self.plan(r, True)
            for i in range(1 << len(bits)):
                self.pack(offset + i, base + spread(i, bits))
        else:
            for d, mask in enumerate(self.masks):
                self.pack(self.offset + d, self.k.q ^ mask)
            self.across.start()
        for link in self.links[r]:
            link.start()

    def step(self):
        if self.now == self.rounds - 1:
            return
        k = self.k
        base, bits, offset = self.plan(self.now, False)
        self.links[self.now][0].arrive()
        for i in range(1 << len(bits)):
            rows = self.rows(base + spread(i, bits))
            got = self.rcv[offset + i].reshape(2 * k.unit, self.cols)
            self.acc[rows, self.lanes] += got.astype(F32)
        self.now += 1
        self.send()

    def end(self):
        while self.now < self.rounds - 1:
            self.step()
        k = self.k
        for arrival in self.arrivals:
            arrival.wait_recv()
        self.across.arrive()
        mine, theirs = self.acc[self.at_core(k.q, k.c), self.lanes], self.core[...]
        for d in range(len(self.masks)):
            mine = mine + self.last[2 * d + k.c].astype(F32)
            theirs = theirs + self.last[2 * d + 1 - k.c].astype(F32)
        for core, value in ((k.c, mine), (1 - k.c, theirs)):
            self.out[:, pl.ds(pl.multiple_of(self.place(core), self.cols), self.cols)] = value


class Device:
    def __init__(self, chips, unit, sems):
        self.chips, self.unit, self.sems = chips, unit, sems
        self.p = lax.axis_index("space")
        self.c = lax.rem(self.p, 2)
        self.q = self.p // 2
        self.used = 0
        self.links = []

    def bit(self, b):
        return lax.rem(self.q // (1 << b), 2)

    def sem(self, count=1):
        self.used += count
        assert self.used <= self.sems.shape[0]
        return self.used - count

    def arrival(self, ref, sem):
        return pltpu.make_async_remote_copy(
            src_ref=ref,
            dst_ref=ref,
            send_sem=self.sems.at[sem],
            recv_sem=self.sems.at[sem],
            device_id={"space": self.p ^ 1},
            device_id_type=pl.DeviceIdType.MESH,
        )

    def fetch(self, src, dst):
        copy = pltpu.make_async_copy(src, dst, self.sems.at[self.sem()])
        copy.start()
        return copy

    def finish(self):
        for link in self.links:
            if link.started and not link.gone:
                link.leave(None if link.left_if is None else jnp.logical_not(link.left_if))


def kernel(
    chips, normalizer,
    g_ref, x_ref, h2_ref, h1_ref, w3_ref, gw_ref, w1_ref,
    in_ref, third_ref, group_ref, first_ref,
    g, x, h2, h1, w3, gw, w1, inner, shifted, first, other, xt, h1t, dense, taps_t,
    acc_t, acc_f, acc_g, snd_t, rcv_t, last_t, core_t, snd_f, rcv_f, last_f, core_f,
    snd_g, rcv_g, piece_g, last_g, snd_r, rcv_r, piece_r, last_r, core_g, out_t, out_f, out_g, out_in, sems,
):
    tall, wide, channels = g_ref.shape
    unit = third_ref.shape[0]
    block = h1.shape[-1]
    half = block // 2
    width = 2 * wide
    size = tall * width
    taps = gw.shape[1]
    gap = taps // 9
    bits = chips.bit_length() - 1
    k = Device(chips, unit, sems)
    p, c, q = k.p, k.c, k.q
    a = k.bit(0)
    even, odd = a == 0, a == 1
    has_up, has_down = q > 0, q < chips - 1

    def lanes(j, core):
        return pl.ds(pl.multiple_of((2 * j + core) * block, block), block)

    order = [0, tall - 1] + list(range(1, tall - 1))
    load_g = {y: k.fetch(g_ref.at[y], g.at[y, c]) for y in order}
    load_w3 = [k.fetch(w3_ref.at[lanes(j, c)], w3.at[j]) for j in (0, 1)]
    load_h2 = {y: k.fetch(h2_ref.at[y], h2.at[y, c]) for y in order}

    barrier = pltpu.get_barrier_semaphore()
    friends = [p ^ 1]
    for b in range(bits):
        friends += [p ^ (2 << b), p ^ (2 << b) ^ 1]
    far = 3 << (bits - 1)
    friends += [p ^ far, p ^ far ^ 1]

    def greet(there):
        pl.semaphore_signal(barrier, inc=1, device_id={"space": there}, device_id_type=pl.DeviceIdType.MESH)

    for there in friends:
        greet(there)
    outer = jnp.where(even, p - 2, p + 2)
    has_outer = jnp.where(even, q > 0, q < chips - 1)
    run(functools.partial(greet, outer), has_outer)

    def inner_tile(rows, tile):
        side = pl.ds(pl.multiple_of(tile * wide, wide), wide)
        left = jnp.concatenate([g[y, tile] for y in rows], 0)
        for j in (0, 1):
            back = dot(left, w3[j], NT)
            for i, y in enumerate(rows):
                mask = h2[y, tile, :, lanes(j, c)]
                part = back[i * wide : (i + 1) * wide]
                inner[j, y + 1, side, :] = jnp.where(mask > 0, part, 0.0).astype(BF)

    pl.semaphore_wait(barrier, len(friends) + jnp.where(has_outer, 1, 0))

    link_h1 = [
        Link(k, h1_ref.at[pl.ds((1 - a) * tall + at, rows)], h1.at[a, pl.ds(at, rows)], p ^ 2)
        for at, rows in ((1, tall - 2), (0, 1), (tall - 1, 1))
    ]
    link_g = {y: Link(k, g_ref.at[y], g.at[y, c], p ^ 1) for y in order}
    link_h2 = {y: Link(k, h2_ref.at[y], h2.at[y, c], p ^ 1) for y in order}
    link_x = Link(k, x_ref, x.at[:, c], p ^ 1)
    def edge(j, source, target, there, goes, comes, tile):
        side = pl.ds(pl.multiple_of(tile * wide, wide), wide)
        return Link(k, inner.at[j, source, side], inner.at[j, target, side], there, goes, comes)

    halos = [
        [
            [
                edge(j, 1, tall + 1, p - 2, has_up, has_down, tile),
                edge(j, tall, 0, p + 2, has_down, has_up, tile),
            ]
            for tile in (c, 1 - c)
        ]
        for j in (0, 1)
    ]

    for y in order[:2]:
        link_g[y].start()
        link_h2[y].start()
    link_h1[0].start()
    for y in order[2:]:
        link_g[y].start()
        link_h2[y].start()
    for copy in load_w3:
        copy.wait()
    for y in order[:2]:
        load_g[y].wait()
        load_h2[y].wait()
    inner_tile(order[:2], c)
    for link in halos[0][0]:
        link.start()
    for y in order[:2]:
        link_g[y].arrive()
        link_h2[y].arrive()
    inner_tile(order[:2], 1 - c)
    for link in halos[0][1]:
        link.start()
    load_x = k.fetch(x_ref, x.at[:, c])
    link_x.start()
    load_gw = [k.fetch(gw_ref.at[:, lanes(j, c)], gw.at[j]) for j in (0, 1)]
    load_h1 = k.fetch(h1_ref.at[pl.ds(a * tall, tall)], h1.at[a])
    load_w1 = k.fetch(w1_ref, w1)
    for y in order[2:]:
        load_g[y].wait()
        load_h2[y].wait()
    inner_tile(order[2:], c)
    for y in order[2:]:
        link_g[y].arrive()
        link_h2[y].arrive()
    inner_tile(order[2:], 1 - c)

    low = list(range(1, bits)) + [0]
    high = list(range(1, bits))[::-1] + [0]
    early_routes = ((low, False), (list(range(bits)), True))
    late_routes = ((list(range(bits)), True), (list(range(bits)), True))

    third = [
        Sums(k, acc_t.at[j], 0, snd_t.at[j], rcv_t.at[j], last_t.at[j], core_t.at[j], route, False, out_t,
             functools.partial(lambda j, core: (2 * j + core) * block, j))
        for j, route in ((0, low), (1, high))
    ]
    for at in range(0, channels, block):
        left = h2[:, :, :, at : at + block].reshape(size, block).T
        for j in (0, 1):
            right = g[:, :, :, lanes(j, c)].reshape(size, block)
            acc_t[j, at : at + block, :] = dot(left, right) * normalizer
    third[0].send()
    third[1].send()

    load_x.wait()
    link_x.arrive()
    for at in range(0, channels, block):
        xt[at : at + block, :] = x[:, :, :, at : at + block].reshape(size, block).T

    own = (
        lax.broadcasted_iota(jnp.int32, (block, block), 0) // gap
        == lax.broadcasted_iota(jnp.int32, (block, block), 1) // gap
    )
    for j in (0, 1):
        load_gw[j].wait()
        for tap in range(9):
            part = gw[j, tap * gap : (tap + 1) * gap, :].astype(F32)
            full = jnp.concatenate([part] * (block // gap), 0)
            dense[j, tap] = jnp.where(own, full, 0.0).astype(BF)

    column = lax.broadcasted_iota(jnp.int32, (width, block), 0)

    def shift_row(j, y):
        piece = inner[j, y]
        wider = piece.astype(F32)
        before = jnp.where(column == width - 1, 0.0, pltpu.roll(wider, width - 1, 0))
        after = jnp.where(column == 0, 0.0, pltpu.roll(wider, 1, 0))
        at = slice(y * width, (y + 1) * width)
        shifted[j, 0, at, :] = before.astype(BF)
        shifted[j, 1, at, :] = piece
        shifted[j, 2, at, :] = after.astype(BF)

    for j in (0, 1):
        for y in range(1, tall + 1):
            shift_row(j, y)
    taps_t[...] = jnp.zeros_like(taps_t)

    def first_sums(j, h, route):
        i = 2 * j + h
        return Sums(k, acc_f.at[j], h * half, snd_f.at[i], rcv_f.at[i], last_f.at[i], core_f.at[i], *route, out_f,
                    functools.partial(lambda j, h, core: (2 * j + core) * block + h * half, j, h))

    early = [first_sums(0, h, route) for h, route in enumerate(early_routes)]
    late = [first_sums(1, h, route) for h, route in enumerate(late_routes)]
    link_first = [Link(k, first.at[j, :, 1 - c], other.at[j], p ^ 1) for j in (0, 1)]

    top = q // (chips // 4)
    below = lax.rem(q, chips // 4)
    low_bits = list(range(bits - 2))

    def group_rows(chip, core=None):
        if core is None:
            return pl.ds(pl.multiple_of(chip * 2 * unit, 2 * unit), 2 * unit)
        return pl.ds(pl.multiple_of((2 * chip + core) * unit, unit), unit)

    def group_plan(r, other):
        b, rest = low_bits[r], low_bits[r + 1 :]
        base = sum(k.bit(d) * (1 << d) for d in low_bits[:r])
        base = base + (1 - k.bit(b) if other else k.bit(b)) * (1 << b)
        return base, rest, chips // 4 - (1 << (len(low_bits) - r))

    whole = snd_g.shape[-1]
    fold = snd_r.shape[-1] // (taps - whole)
    few = unit // fold

    def split(part):
        part = part.reshape(2, unit, taps)
        rest = [part[:, i * few : (i + 1) * few, whole:] for i in range(fold)]
        return part[:, :, :whole].astype(BF), jnp.concatenate(rest, 2).astype(BF)

    def joined(main, rest):
        rest = rest.astype(F32)
        step = taps - whole
        rest = [rest[..., i * step : (i + 1) * step] for i in range(fold)]
        return main.astype(F32), jnp.concatenate(rest, rest[0].ndim - 2)

    link_group = {}
    for j in (0, 1):
        for r, b in enumerate(low_bits):
            _, rest, offset = group_plan(r, True)
            span = pl.ds(offset, 1 << len(rest))
            link_group[j, r] = [
                Link(k, snd.at[j, span], rcv.at[j, span], p ^ (2 << b)) for snd, rcv in ((snd_g, rcv_g), (snd_r, rcv_r))
            ]
    group_base = k.sem(8)
    group_arrivals = [
        [k.arrival(last.at[t], group_base + 4 * i + t) for i, last in enumerate((last_g, last_r))] for t in range(4)
    ]
    group_across_sem = k.sem()
    group_across_arrival = k.arrival(core_g, group_across_sem)
    link_last, link_across = [], []
    for j in (0, 1):
        owner = 2 * j + c
        link_last.append(
            [
                Link(k, piece.at[j, core], last.at[top], 2 * (owner * (chips // 4) + below) + core,
                     goes=owner != top, receive=group_base + 4 * i + top)
                for core in (0, 1)
                for i, (piece, last) in enumerate(((piece_g, last_g), (piece_r, last_r)))
            ]
        )
        link_across.append(
            Link(k, acc_g.at[j, group_rows(below, 1 - c)], core_g, p ^ 1, goes=owner == top, receive=group_across_sem)
        )

    def group_send(j, r):
        base, rest, offset = group_plan(r, True)
        for i in range(1 << len(rest)):
            main, past = split(acc_g[j, group_rows(base + spread(i, rest)), :])
            snd_g[j, offset + i] = main
            snd_r[j, offset + i] = past
        for link in link_group[j, r]:
            link.start()

    def group_receive(j, r):
        base, rest, offset = group_plan(r, False)
        for link in link_group[j, r]:
            link.arrive()
        for i in range(1 << len(rest)):
            main, past = joined(rcv_g[j, offset + i], rcv_r[j, offset + i])
            rows = group_rows(base + spread(i, rest))
            acc_g[j, rows, :whole] += main.reshape(2 * unit, whole)
            acc_g[j, rows, whole:] += past.reshape(2 * unit, taps - whole)

    def group_onward(j):
        for r in range(len(low_bits)):
            group_receive(j, r)
            if r + 1 < len(low_bits):
                group_send(j, r + 1)
        piece_g[j], piece_r[j] = split(acc_g[j, group_rows(below), :])
        for link in (*link_last[j], link_across[j]):
            link.start()

    def conv_row(j, y):
        total = None
        for tap in range(9):
            u, v = tap // 3 - 1, tap % 3 - 1
            rows = (y + 1 - u) * width
            rows = pl.ds(rows if isinstance(y, int) else pl.multiple_of(rows, width), width)
            term = dot(shifted[j, v + 1, rows, :], dense[j, tap], NT)
            total = term if total is None else total + term
        result = jnp.where(h1[j, y] > 0, total, 0.0).astype(BF)
        first[j, y] = result.reshape(2, wide, block)

    def conv_inside(j):
        run(load_h1.wait, a == j)
        run(link_h1[0].copy.wait_recv, a != j)

        @pl.loop(1, tall - 1)
        def _(y):
            conv_row(j, y)

        for at in range(0, channels, block):
            right = first[j, 1 : tall - 1].reshape(size - 2 * width, block)
            left = xt[at : at + block, width : size - width]
            acc_f[j, at : at + block, :] = dot(left, right) * normalizer

    def conv_edges(j, pieces):
        for links in halos[j]:
            for link in links:
                link.arrive()
        for there, target in ((has_down, tall + 1), (has_up, 0)):

            @pl.when(jnp.logical_not(there))
            def _(target=target):
                inner[j, target] = jnp.zeros((width, block), BF)

        for link in link_h1[1:]:
            run(link.copy.wait_recv, a != j)
        shift_row(j, 0)
        shift_row(j, tall + 1)
        for y in (0, tall - 1):
            conv_row(j, y)
        for at in range(0, channels, block):
            term = None
            for y in (0, tall - 1):
                left = xt[at : at + block, y * width : (y + 1) * width]
                part = dot(left, first[j, y].reshape(width, block))
                term = part if term is None else term + part
            acc_f[j, at : at + block, :] += term * normalizer
        for piece in pieces:
            piece.send()
        link_first[j].start()

    def conv_weights(j):
        for y in range(tall):
            h1t[:, y * width : (y + 1) * width] = h1[j, y].T
        for tap in range(9):
            u, v = tap // 3 - 1, tap % 3 - 1
            at = (1 - u) * width
            term = dot(h1t[...], shifted[j, v + 1, at : at + size, :])
            term = jnp.where(own, term, 0.0)
            folded = term[:gap]
            for i in range(1, block // gap):
                folded = folded + term[i * gap : (i + 1) * gap]
            taps_t[tap * gap : (tap + 1) * gap, :] = folded * normalizer
        acc_g[j] = taps_t[...].T[:, :taps]
        if low_bits:
            group_send(j, 0)

    def input_gradient():
        load_w1.wait()
        total = g[:, c].reshape(tall * wide, channels).astype(F32)
        for j in (0, 1):
            link_first[j].arrive()
            total = total + dot(first[j, :, c].reshape(tall * wide, block), w1[:, lanes(j, c)], NT)
            total = total + dot(other[j].reshape(tall * wide, block), w1[:, lanes(j, 1 - c)], NT)
        out_in[...] = total.astype(BF).reshape(tall, wide, channels)
        return k.fetch(out_in, in_ref)

    def group_end():
        for t in range(4):
            for arrival in group_arrivals[t]:
                run(arrival.wait_recv, top != t)
        holder = lax.rem(top, 2)

        @pl.when(holder == c)
        def _():
            out_g[...] = acc_g[top // 2, group_rows(below, c), :]

        @pl.when(holder != c)
        def _():
            group_across_arrival.wait_recv()
            out_g[...] = core_g[...]

        for t in range(4):

            @pl.when(top != t)
            def _(t=t):
                main, past = joined(last_g[t], last_r[t])
                out_g[:, :whole] += main
                out_g[:, whole:] += past

        return k.fetch(out_g, group_ref)

    stores = []
    for link in (*halos[0][0], *halos[0][1]):
        link.leave(also=odd)
    for link in (*halos[1][0], *halos[1][1], *link_h1[1:]):
        link.start(also=odd)
    link_h1[0].leave(also=even)
    for link in link_h1[1:]:
        link.start(also=even)
    conv_inside(1)
    conv_inside(0)
    conv_edges(0, early)
    for link in link_h1[1:]:
        link.leave(also=even)
    for link in (*halos[1][0], *halos[1][1]):
        link.start(also=even)

    for piece in third:
        piece.step()
    conv_weights(0)
    conv_edges(1, late)
    for piece in early:
        piece.step()
    conv_weights(1)
    for r in range(1, bits):
        for piece in late + third + early:
            piece.step()
        if r == 1:
            group_onward(0)
            group_onward(1)
    stores.append(input_gradient())

    for piece in third:
        piece.end()
    stores.append(k.fetch(out_t, third_ref))
    for piece in early + late:
        piece.end()
    stores.append(k.fetch(out_f, first_ref))
    stores.append(group_end())
    k.finish()
    for copy in stores:
        copy.wait()


def hand_over(*refs):
    sources, targets, held, sems = refs[:4], refs[4:8], refs[8:12], refs[12]
    moves = []
    for source, target, place in zip(sources, targets, held):
        pieces = range(source.shape[0]) if len(source.shape) == 3 else [slice(None)]
        for piece in pieces:
            at = len(moves)
            moves.append(
                (
                    pltpu.make_async_copy(source.at[piece], place.at[piece], sems.at[0, at]),
                    pltpu.make_async_copy(place.at[piece], target.at[piece], sems.at[1, at]),
                )
            )
    for load, _ in moves:
        load.start()
    for load, store in moves:
        load.wait()
        store.start()
    for _, store in moves:
        store.wait()


def per_device(
    outer_grad, block_input, third_input, second_input, third_weight, group_weight, first_weight
):
    devices = lax.axis_size("space")
    chips = devices // 2
    _, tall, wide, channels = outer_grad.shape
    block = second_input.shape[3]
    taps = group_weight.shape[1]
    unit = channels // devices
    width, size = 2 * wide, 2 * tall * wide
    half = block // 2
    normalizer = 1.0 / math.sqrt(tall * wide * devices)
    padded = -(-taps // 128) * 128
    whole = taps // 128 * 128
    fold = max(1, min(128 // (taps - whole), unit // 16))
    past = fold * (taps - whole)
    anywhere = pl.BlockSpec(memory_space=pl.ANY)

    def vmem(*shape, dtype=BF):
        return pltpu.VMEM(shape, dtype)

    scratch = [
        vmem(tall, 2, wide, channels),
        vmem(tall, 2, wide, channels),
        vmem(tall, 2, wide, channels),
        vmem(2, tall, width, block),
        vmem(2, block, channels),
        vmem(2, taps, block),
        vmem(channels, channels),
        vmem(2, tall + 2, width, block),
        vmem(2, 3, (tall + 2) * width, block),
        vmem(2, tall, 2, wide, block),
        vmem(2, tall, wide, block),
        vmem(channels, size),
        vmem(block, size),
        vmem(2, 9, block, block),
        vmem(padded, block, dtype=F32),
        vmem(2, channels, block, dtype=F32),
        vmem(2, channels, block, dtype=F32),
        vmem(2, block, taps, dtype=F32),
        vmem(2, chips, 2, unit, block),
        vmem(2, chips, 2, unit, block),
        vmem(2, 2, unit, block),
        vmem(2, unit, block, dtype=F32),
        vmem(4, chips, 2, unit, half),
        vmem(4, chips, 2, unit, half),
        vmem(4, 6, unit, half),
        vmem(4, unit, half, dtype=F32),
        vmem(2, max(chips // 4, 1), 2, unit, whole),
        vmem(2, max(chips // 4, 1), 2, unit, whole),
        vmem(2, 2, unit, whole),
        vmem(4, unit, whole),
        vmem(2, max(chips // 4, 1), 2, unit // fold, past),
        vmem(2, max(chips // 4, 1), 2, unit // fold, past),
        vmem(2, 2, unit // fold, past),
        vmem(4, unit // fold, past),
        vmem(unit, taps, dtype=F32),
        vmem(unit, channels, dtype=F32),
        vmem(unit, channels, dtype=F32),
        vmem(unit, taps, dtype=F32),
        vmem(tall, wide, channels),
        pltpu.SemaphoreType.DMA((256,)),
    ]
    input_grad, third_wgrad, group_wgrad, first_wgrad = pl.pallas_call(
        functools.partial(kernel, chips, normalizer),
        in_specs=[anywhere] * 7,
        out_specs=[anywhere] * 4,
        out_shape=[
            jax.ShapeDtypeStruct((tall, wide, channels), BF),
            jax.ShapeDtypeStruct((unit, channels), F32),
            jax.ShapeDtypeStruct((unit, taps), F32),
            jax.ShapeDtypeStruct((unit, channels), F32),
        ],
        scratch_shapes=scratch,
        compiler_params=pltpu.CompilerParams(
            collective_id=0, has_side_effects=True, vmem_limit_bytes=56 * 2**20
        ),
        cost_estimate=pl.CostEstimate(
            flops=9 * 10**9, bytes_accessed=12 * 2**20, transcendentals=0
        ),
    )(
        outer_grad[0],
        block_input[0],
        third_input[0],
        second_input[0],
        third_weight,
        group_weight.T,
        first_weight,
    )
    results = (input_grad, third_wgrad, group_wgrad, first_wgrad)
    results = pl.pallas_call(
        hand_over,
        in_specs=[anywhere] * 4,
        out_specs=[anywhere] * 4,
        out_shape=[jax.ShapeDtypeStruct(r.shape, r.dtype) for r in results],
        scratch_shapes=[pltpu.VMEM(r.shape, r.dtype) for r in results] + [pltpu.SemaphoreType.DMA((2, tall + 3))],
    )(*results)
    return results[0][None], results[1], results[2], results[3]


def solution(mesh):
    spread_out = P(("parts", "space"), None, None, None)
    rows = P(("parts", "space"), None)
    return jax.shard_map(
        per_device,
        mesh=mesh,
        in_specs=(spread_out,) * 4 + (P(),) * 3,
        out_specs=(spread_out, rows, rows, rows),
        check_vma=False,
    )
```
